32 devices in a mesh: layer: 2 (over x), row: 4 (over z), col: 4 (over y, core).
Axes of the slice: x: 2, y: 2, z: 4, core: 2. Of those that a mesh axis runs over, the one named last changes fastest.
Arguments:
- query_weight: bfloat16 [32768, 16384], P(('layer', 'row'), 'col'), parts along dimension 0, may hold values from -0.046875 to 0.046875
- sign_input: int32 [32768], P(('layer', 'col')), parts along dimension 0, may hold values from -1 to 1, as said below
- sign_output: int32 [32768], P(('layer', 'row')), parts along dimension 0, may hold values from -1 to 1, as said below
- clip_level: int32 [256, 128], P(('layer', 'row'), 'col'), parts along dimension 0, may hold values from 1 to 8
- calibration: bfloat16 [768, 16384], P(('layer', 'row'), 'col'), parts along dimension 0, may hold values from -6 to 6
Outputs:
- projected: bfloat16 [768, 16384], P(('layer', 'col'), 'row'), parts along dimension 0
The draws below stay inside these ranges and needn't reach their ends.
There are 2 independent parts, one for each index of `layer`. The reference program is written for one: setup_inputs(seed, part) draws one part's arguments, and reference() takes and returns one part's arrays. A program takes and returns all parts, laid end to end along the dimension named above; each array names one. Nothing has to cross between parts.
Inputs may be any that keep to these rules, and one draw needn't show every extreme that they name: `sign_input`: every entry is -1 or 1. `sign_output`: every entry is -1 or 1.
All inputs are finite; a program needn't handle non-finite values.
Results may differ from the reference program's by a relative error of at most 0.0064.
Values may be sent and summed in bfloat16 or wider, within the bound.
A program may use at most 256 MiB of HBM per device.

```python
import jax
import jax.numpy as jnp
from jax import lax

OUTER = 16
INNER = 1024
D = 16384
BLK = 128
CAL = 384


def draw_sign_input(key, part):
    coin_flips = jax.random.randint(jax.random.fold_in(key, 11), (D,), 0, 2)
    return (2 * coin_flips - 1).astype(jnp.int32)


def draw_sign_output(key, part):
    coin_flips = jax.random.randint(jax.random.fold_in(key, 12), (D,), 0, 2)
    return (2 * coin_flips - 1).astype(jnp.int32)


def set_ends(result, own_key, low, high):
    longest = result.shape.index(max(result.shape))
    spots = []
    for shift in (0, 1):
        where = [jax.random.randint(jax.random.fold_in(own_key, axis), (), 0, length) for axis, length in enumerate(result.shape)]
        where[longest] = (where[longest] + shift) % result.shape[longest]
        spots.append(tuple(where))
    return result.at[spots[0]].set(low).at[spots[1]].set(high)


def steps_of(own_key, shape, cuts, least, largest):
    level = 1.0
    for axis_at, parts in cuts:
        steps = jax.random.uniform(jax.random.fold_in(jax.random.fold_in(own_key, 6), axis_at), (parts,), jnp.float32, least / len(cuts), largest / len(cuts))
        level = level * jnp.repeat(jnp.exp(steps), shape[axis_at] // parts).reshape((-1,) + (1,) * (len(shape) - 1 - axis_at))
    return level


def centred(own_key, dims, scale, reach, shards=(), held_as=jnp.bfloat16):
    array = jax.random.normal(own_key, dims, jnp.float32) * scale
    if len(shards) > 0:
        array = steps_of(own_key, dims, shards, -0.22, 0.18) * array
    return jnp.clip(array, min=-reach, max=reach).astype(held_as)


def setup_inputs(seed: int = 0, part: int = 0) -> dict:
    key_list = jax.random.split(jax.random.key(seed), 6)
    part_splits = jax.random.split(jax.random.fold_in(key_list[5], part), 6)
    query_weight = centred(part_splits[0], (D, D), D ** -0.5, 0.046875, ((0, 4), (1, 4)))
    sign_input = draw_sign_input(jax.random.fold_in(jax.random.fold_in(key_list[5], part), 71), part)
    sign_output = draw_sign_output(jax.random.fold_in(jax.random.fold_in(key_list[5], part), 71), part)
    clip_level = set_ends(jax.random.randint(part_splits[3], (D // BLK, D // BLK), 1, 9), jax.random.fold_in(part_splits[3], 1), 1, 8).astype(jnp.int32)
    calibration = centred(part_splits[4], (CAL, D), 1.0, 6.0, ((0, 4), (1, 4)))
    return dict(query_weight=query_weight, sign_input=sign_input, sign_output=sign_output, clip_level=clip_level, calibration=calibration)


def sylvester(length):
    indices = jnp.arange(length, dtype=jnp.int32)
    common_bits = indices[:, None] & indices[None, :]
    parity_sum = jnp.zeros((length, length), jnp.int32)
    for bit_number in range(max(length.bit_length() - 1, 1)):
        parity_sum = parity_sum ^ ((common_bits >> bit_number) & 1)
    return (1 - 2 * parity_sum).astype(jnp.float32)


def inner_right(weights, sign_vector, inner_size):
    row_total, col_total = weights.shape
    groups = inner_size // 128
    lane_table = jnp.asarray(sylvester(128), jnp.float32)
    mixing = jnp.asarray(sylvester(groups), jnp.float32)
    signed = weights.astype(jnp.float32) * sign_vector.astype(jnp.float32)[None, :]
    shaped = signed.reshape(row_total, col_total // inner_size, groups, 128)
    partial_sum = jnp.einsum('rage,ef->ragf', shaped, lane_table, precision=lax.Precision.HIGHEST)
    mixed = jnp.einsum('gh,rahf->ragf', mixing, partial_sum, precision=lax.Precision.HIGHEST)
    return mixed.reshape(row_total, col_total).astype(jnp.bfloat16)


def inner_left(weights, sign_vector, inner_size):
    row_total, col_total = weights.shape
    groups = inner_size // 128
    lane_table = jnp.asarray(sylvester(128), jnp.float32)
    mixing = jnp.asarray(sylvester(groups), jnp.float32)
    signed = weights.astype(jnp.float32) * sign_vector.astype(jnp.float32)[:, None]
    shaped = signed.reshape(row_total // inner_size, groups, 128, col_total)
    partial_sum = jnp.einsum('ef,cgek->cgfk', lane_table, shaped, precision=lax.Precision.HIGHEST)
    mixed = jnp.einsum('gh,chfk->cgfk', mixing, partial_sum, precision=lax.Precision.HIGHEST)
    return mixed.reshape(row_total, col_total).astype(jnp.bfloat16)


def reference(query_weight, sign_input, sign_output, clip_level, calibration):
    def first_pass(packed):
        rows_block, sign_rows = packed
        right_done = inner_right(rows_block, sign_input, INNER)
        return inner_left(right_done, sign_rows, INNER)

    inner_both = lax.map(first_pass, (query_weight.reshape(OUTER, INNER, D), sign_output.reshape(OUTER, INNER)))
    outer_table = jnp.asarray(sylvester(OUTER), jnp.float32)
    levels = clip_level.astype(jnp.float32) / 512.0

    def second_pass(index):
        def accumulate(source, total):
            return total + outer_table[index, source] * inner_both[source].astype(jnp.float32)

        mixed_rows = lax.fori_loop(0, OUTER, accumulate, jnp.zeros((INNER, D), jnp.float32))
        shaped = mixed_rows.reshape(INNER, OUTER, INNER)
        rotated = jnp.einsum('ak,dkb->dab', outer_table, shaped, precision=lax.Precision.HIGHEST).reshape(INNER, D) / D
        limit_rows = lax.dynamic_slice_in_dim(levels, (index * (INNER // BLK)).astype(jnp.int32), INNER // BLK, 0)
        limit_full = jnp.repeat(jnp.repeat(limit_rows, BLK, 0), BLK, 1)
        clipped = jnp.clip(rotated, -limit_full, limit_full).astype(jnp.bfloat16)
        return lax.dot_general(calibration, clipped, (((1,), (1,)), ((), ())), preferred_element_type=jnp.float32)

    pieces = lax.map(second_pass, jnp.arange(OUTER, dtype=jnp.int32))
    return jnp.transpose(pieces, (1, 0, 2)).reshape(CAL, D).astype(jnp.bfloat16)
```

```python
import functools

import jax
import jax.numpy as jnp
from jax import lax
from jax.experimental import pallas as pl
from jax.experimental.pallas import tpu as pltpu
from jax.sharding import PartitionSpec as P

INNER = 1024
D = 16384
BLK = 128
LEVEL_UNIT = 512
GROUP = 256
SEND_SLOTS = 3
WEIGHT_SLOTS = 3
MESH = pl.DeviceIdType.MESH


def bits_of(size):
    bits = []
    while size > 1:
        size //= 2
        bits.append(size)
    return bits


def flip(at, bit):
    return at + bit * (1 - 2 * lax.rem(at // bit, 2))


def exclusive_or(a, b, size):
    total = 0
    for bit in bits_of(size):
        total = total + bit * lax.rem(a // bit + b // bit, 2)
    return total


def sylvester(size):
    x = lax.broadcasted_iota(jnp.int32, (size, size), 0) & lax.broadcasted_iota(jnp.int32, (size, size), 1)
    x = x ^ (x >> 4)
    x = x ^ (x >> 2)
    x = x ^ (x >> 1)
    return (1 - 2 * (x & 1)).astype(jnp.float32)


def butterfly(values):
    values = list(values)
    half = 1
    while half < len(values):
        for at in range(len(values)):
            if not at & half:
                low, high = values[at], values[at + half]
                values[at], values[at + half] = low + high, low - high
        half *= 2
    return values


def kernel(
    R, C, w_ref, si_ref, so_ref, level_ref, cal_ref, recv_ref, out_ref,
    kout, skin, kin, wbuf, right, sbuf, rbuf, mix, clip, acc, accb, perm, calv, levv, levb, lim, ostage,
    wsem, ssem, own_sem, rsem, usem, cal_own, cal_send, cal_recv, lev_send, lev_recv, out_send, out_recv,
):
    layer, r, c = lax.axis_index("layer"), lax.axis_index("row"), lax.axis_index("col")
    n = R * C
    me = r * C + c
    units, _, ob, ds, wide = recv_ref.shape
    ib = wide // BLK
    chunks = INNER // BLK
    S = units // chunks
    pr = S * ds
    ao, ai = R * ob, C * ib
    groups = INNER // BLK
    blocks = ob * ib
    lev_cols = level_ref.shape[1]
    row_bits, col_bits = bits_of(R), bits_of(C)
    stages = len(row_bits) + len(col_bits)

    def peer(i):
        pr_, pc_ = exclusive_or(r, i // C, R), exclusive_or(c, lax.rem(i, C), C)
        return (layer, pr_, pc_), pr_ * C + pc_

    def w_copy(q):
        block, slot = lax.rem(q, blocks), lax.rem(q, WEIGHT_SLOTS)
        rows = pl.ds(pl.multiple_of((block // ib) * INNER, INNER), INNER)
        cols = pl.ds(pl.multiple_of(lax.rem(block, ib) * INNER, INNER), INNER)
        return pltpu.make_async_copy(w_ref.at[rows, cols], wbuf.at[slot], wsem.at[slot])

    def cal_slot(rr, cc):
        slot, weight = 0, 1
        for bit in row_bits:
            slot = slot + weight * lax.rem(r // bit + rr // bit, 2)
            weight *= 2
        for bit in col_bits:
            slot = slot + weight * lax.rem(c // bit + cc // bit, 2)
            weight *= 2
        return slot

    def cal_copy(stage):
        size = 2**stage
        if stage < len(row_bits):
            target = (layer, flip(r, row_bits[stage]), c)
        else:
            target = (layer, r, flip(c, col_bits[stage - len(row_bits)]))
        return pltpu.make_async_remote_copy(
            src_ref=cal_ref if stage == 0 else calv.at[pl.ds(0, size)],
            dst_ref=calv.at[1] if stage == 0 else calv.at[pl.ds(size, size)],
            send_sem=cal_send.at[stage],
            recv_sem=cal_recv.at[stage],
            device_id=target,
            device_id_type=MESH,
        )

    cal_own_copy = pltpu.make_async_copy(cal_ref, calv.at[0], cal_own)

    def cal_advance(stage):
        if stage >= stages:
            return
        if stage == 0:
            cal_own_copy.wait()
        cal_copy(stage).wait_recv()
        if stage + 1 < stages:
            cal_copy(stage + 1).start()

    barrier = pltpu.get_barrier_semaphore()

    @pl.loop(1, n)
    def _(i):
        target, _ = peer(i)
        pl.semaphore_signal(barrier, inc=1, device_id=target, device_id_type=MESH)

    cal_own_copy.start()
    for q in range(WEIGHT_SLOTS - 1):
        w_copy(q).start()
    pl.semaphore_wait(barrier, n - 1)

    if stages:
        cal_copy(0).start()
    pltpu.make_async_copy(level_ref, levv.at[me], lev_recv).start()

    @pl.loop(1, n)
    def _(i):
        target, _ = peer(i)
        pltpu.make_async_remote_copy(
            src_ref=level_ref, dst_ref=levv.at[me], send_sem=lev_send, recv_sem=lev_recv,
            device_id=target, device_id_type=MESH,
        ).start()

    table = sylvester(BLK)
    table_b = table.astype(jnp.bfloat16)
    diagonal = lax.broadcasted_iota(jnp.int32, (BLK, BLK), 0) == lax.broadcasted_iota(jnp.int32, (BLK, BLK), 1)

    def static_sign(a, b):
        return 1.0 - 2.0 * (bin(a & b).count("1") & 1)

    @pl.loop(0, ib)
    def _(k):
        for g in range(groups):
            signs = si_ref[k, :, g * BLK : (g + 1) * BLK].astype(jnp.float32)
            scaled = jnp.where(diagonal, signs, 0.0).astype(jnp.bfloat16)
            skin[k, g * BLK : (g + 1) * BLK, :] = jnp.dot(
                scaled, table_b, preferred_element_type=jnp.float32
            ).astype(jnp.bfloat16)

    @pl.loop(0, ob)
    def _(j):
        for g in range(groups):
            signs = so_ref[j, :, g * BLK : (g + 1) * BLK].astype(jnp.float32)
            plus = (table * signs).astype(jnp.bfloat16)
            minus = (table * -signs).astype(jnp.bfloat16)
            for h in range(groups):
                kout[j, h * BLK : (h + 1) * BLK, g * BLK : (g + 1) * BLK] = plus if static_sign(g, h) > 0 else minus

    def inner(t, slot):
        for g in range(groups):
            parity = 0
            for bit in bits_of(groups):
                if g & bit:
                    parity = parity + lax.rem(t // bit, 2)
            sign = (1 - 2 * lax.rem(parity + 0 * t, 2)).astype(jnp.float32)
            for k in range(ib):
                rows = slice(g * BLK, (g + 1) * BLK)
                kin[k, rows, :] = (skin[k, rows, :].astype(jnp.float32) * sign).astype(jnp.bfloat16)

        @pl.loop(0, ob)
        def _(j):
            @pl.loop(0, ib)
            def _(k):
                q = (t * ob + j) * ib + k
                w_copy(q).wait()

                @pl.when(q + WEIGHT_SLOTS - 1 < chunks * blocks)
                def _():
                    w_copy(q + WEIGHT_SLOTS - 1).start()

                wslot = lax.rem(q, WEIGHT_SLOTS)

                @pl.loop(0, INNER // GROUP)
                def _(m):
                    rows = pl.ds(pl.multiple_of(m * GROUP, GROUP), GROUP)
                    cols = pl.ds(pl.multiple_of(k * BLK, BLK), BLK)
                    right[rows, cols] = jnp.dot(
                        wbuf[wslot, rows, :], kin[k], preferred_element_type=jnp.float32
                    ).astype(jnp.bfloat16)

            @pl.loop(0, INNER // GROUP)
            def _(m):
                rows = pl.ds(pl.multiple_of(m * GROUP, GROUP), GROUP)
                both = jnp.dot(kout[j, rows, :], right[...], preferred_element_type=jnp.float32)
                per = GROUP // pr
                sbuf[slot, pl.ds(m * per, per), :, j] = both.reshape(per, S, ds, wide).astype(jnp.bfloat16)

    def send(t, slot):
        @pl.loop(0, S)
        def _(s):
            u = t * S + s
            pltpu.make_async_copy(sbuf.at[slot, me, s], recv_ref.at[u, me], own_sem.at[slot]).start()

            @pl.loop(1, n)
            def _(i):
                target, place = peer(n - i)
                pltpu.make_async_remote_copy(
                    src_ref=sbuf.at[slot, place, s], dst_ref=recv_ref.at[u, me],
                    send_sem=ssem.at[slot], recv_sem=rsem.at[u],
                    device_id=target, device_id_type=MESH,
                ).start()

    def wait_send(slot):
        sent = sbuf.at[slot, pl.ds(0, n - 1)]
        pltpu.make_async_copy(sent, sent, ssem.at[slot]).wait()
        own = sbuf.at[slot, me]
        pltpu.make_async_copy(own, own, own_sem.at[slot]).wait()

    d_block = me * pr // BLK
    d_blocks = INNER // BLK

    def read_levels():
        pltpu.make_async_copy(levv, levv, lev_recv).wait()
        level = levv[...].astype(jnp.float32).reshape(n * ob, d_blocks, lev_cols)
        line = lax.broadcasted_iota(jnp.int32, level.shape, 1)
        level = jnp.sum(jnp.where(line == d_block, level, 0.0), axis=1, keepdims=True)
        level = jnp.broadcast_to(level, (n * ob, d_blocks, lev_cols)).reshape(n * ob * d_blocks, lev_cols)
        levb[...] = level.astype(jnp.bfloat16)

    def outer(t):
        lane = lax.broadcasted_iota(jnp.int32, (lev_cols, wide), 1)
        line = lax.broadcasted_iota(jnp.int32, (lev_cols, wide), 0)
        pick = jnp.where(line == (lane >> 7) * d_blocks + t, float(D // LEVEL_UNIT), 0.0).astype(jnp.bfloat16)
        lim[...] = jnp.dot(levb[...], pick, preferred_element_type=jnp.float32).reshape(lim.shape)

        @pl.loop(0, S)
        def _(s):
            u = t * S + s
            arrived = recv_ref.at[u, pl.ds(0, n - 1)]
            pltpu.make_async_copy(arrived, arrived, rsem.at[u]).wait()
            fetch = pltpu.make_async_copy(recv_ref.at[u], rbuf, usem)
            fetch.start()
            fetch.wait()

            @pl.loop(0, ai)
            def _(i):
                cc, k = i // ib, lax.rem(i, ib)
                cols = pl.ds(pl.multiple_of(k * BLK, BLK), BLK)
                mixed = butterfly(
                    rbuf[rr * C + cc, j, :, cols].astype(jnp.float32) for rr in range(R) for j in range(ob)
                )
                for o in range(ao):
                    mix[i, o] = mixed[o]

            @pl.loop(0, ao)
            def _(o):
                rr, j = o // ob, lax.rem(o, ob)
                mixed = butterfly(mix[i, o] for i in range(ai))
                for i in range(ai):
                    cc, k = i // ib, i % ib
                    limit = lim[(rr * C + cc) * ob + j, :, k * BLK : (k + 1) * BLK]
                    value = mixed[i].reshape(ds // d_blocks, d_blocks, BLK)
                    value = jnp.minimum(jnp.maximum(value, -limit), limit)
                    clip[i, o] = value.reshape(ds, BLK).astype(jnp.bfloat16)

            total = None
            for i in range(ai):
                cc, k = i // ib, i % ib
                cols = pl.ds(pl.multiple_of(k * INNER + t * BLK, BLK), BLK)
                cal = jnp.concatenate([calv[cal_slot(rr, cc), :, cols] for rr in range(R)], axis=0)
                term = lax.dot_general(
                    cal, clip[i].reshape(ao * ds, BLK), (((1,), (1,)), ((), ())), preferred_element_type=jnp.float32
                )
                total = term if total is None else total + term
            acc[s] += total

    spot = lax.broadcasted_iota(jnp.int32, perm.shape[1:], 0)
    lane = lax.broadcasted_iota(jnp.int32, perm.shape[1:], 1)
    shift = pr.bit_length() - 1
    step = ds.bit_length() - 1
    for q in range(R):
        for s in range(S):
            wanted = (q * ob + (lane >> shift)) * ds + (lane & (ds - 1))
            hit = (spot == wanted) & (((lane & (pr - 1)) >> step) == s)
            perm[q * S + s] = jnp.where(hit, 1.0, 0.0).astype(jnp.bfloat16)
    acc[...] = jnp.zeros_like(acc)

    @pl.loop(0, chunks + SEND_SLOTS)
    def _(i):
        slot = lax.rem(i, SEND_SLOTS)

        @pl.when(i >= SEND_SLOTS)
        def _():
            wait_send(slot)

        @pl.when(i < chunks)
        def _():
            inner(i, slot)
            send(i, slot)

        for at in range(SEND_SLOTS + 1):
            @pl.when(i == at)
            def _():
                cal_advance(at)
                if at == SEND_SLOTS:
                    for later in range(at + 1, stages):
                        cal_advance(later)
                    read_levels()

        @pl.when(i >= SEND_SLOTS)
        def _():
            outer(i - SEND_SLOTS)

    accb[...] = (acc[...] * (1.0 / D)).astype(jnp.bfloat16)
    rows_each = ostage.shape[1]

    @pl.loop(0, R)
    def _(q):
        total = None
        for s in range(S):
            term = jnp.dot(accb[s], perm[q * S + s], preferred_element_type=jnp.float32)
            total = term if total is None else total + term
        for cc in range(C):
            ostage[q * C + cc] = total[cc * rows_each : (cc + 1) * rows_each].astype(jnp.bfloat16)

    pltpu.make_async_copy(ostage.at[me], out_ref.at[me], out_recv).start()

    @pl.loop(1, n)
    def _(i):
        target, place = peer(n - i)
        pltpu.make_async_remote_copy(
            src_ref=ostage.at[place], dst_ref=out_ref.at[me], send_sem=out_send, recv_sem=out_recv,
            device_id=target, device_id_type=MESH,
        ).start()

    for stage in range(stages):
        cal_copy(stage).wait_send()
    sent = levv.at[pl.ds(0, n - 1)]
    pltpu.make_async_copy(sent, sent, lev_send).wait()
    pltpu.make_async_copy(out_ref, out_ref, out_recv).wait()
    sent = ostage.at[pl.ds(0, n - 1)]
    pltpu.make_async_copy(sent, sent, out_send).wait()


def shards(query_weight, sign_input, sign_output, clip_level, calibration):
    rows_local, cols_local = query_weight.shape
    R, C = lax.axis_size("row"), lax.axis_size("col")
    n = R * C
    ob, ib = rows_local // INNER, cols_local // INNER
    pr = INNER // n
    ds = min(16, pr)
    S = pr // ds
    chunks = INNER // BLK
    cal_local = calibration.shape[0]
    cal_rows = R * cal_local
    ao, ai = R * ob, C * ib
    wide = ib * BLK
    stages = len(bits_of(R)) + len(bits_of(C))
    bf16, f32 = jnp.bfloat16, jnp.float32

    _, result = pl.pallas_call(
        functools.partial(kernel, R, C),
        in_specs=[
            pl.BlockSpec(memory_space=pl.ANY),
            pl.BlockSpec(memory_space=pltpu.VMEM),
            pl.BlockSpec(memory_space=pltpu.VMEM),
            pl.BlockSpec(memory_space=pl.ANY),
            pl.BlockSpec(memory_space=pl.ANY),
        ],
        out_specs=[pl.BlockSpec(memory_space=pl.ANY)] * 2,
        out_shape=[
            jax.ShapeDtypeStruct((chunks * S, n, ob, ds, wide), bf16),
            jax.ShapeDtypeStruct((n, cal_rows // C, ob * pr), bf16),
        ],
        scratch_shapes=[
            pltpu.VMEM((ob, INNER, INNER), bf16),
            pltpu.VMEM((ib, INNER, BLK), bf16),
            pltpu.VMEM((ib, INNER, BLK), bf16),
            pltpu.VMEM((WEIGHT_SLOTS, INNER, INNER), bf16),
            pltpu.VMEM((INNER, wide), bf16),
            pltpu.VMEM((SEND_SLOTS, n, S, ob, ds, wide), bf16),
            pltpu.VMEM((n, ob, ds, wide), bf16),
            pltpu.VMEM((ai, ao, ds, BLK), f32),
            pltpu.VMEM((ai, ao, ds, BLK), bf16),
            pltpu.VMEM((S, cal_rows, ao * ds), f32),
            pltpu.VMEM((S, cal_rows, ao * ds), bf16),
            pltpu.VMEM((R * S, ao * ds, ob * pr), bf16),
            pltpu.VMEM((n, cal_local, cols_local), bf16),
            pltpu.VMEM((n,) + clip_level.shape, jnp.int32),
            pltpu.VMEM((n * clip_level.shape[0], clip_level.shape[1]), bf16),
            pltpu.VMEM((n * ob, INNER // BLK, wide), f32),
            pltpu.VMEM((n, cal_rows // C, ob * pr), bf16),
            pltpu.SemaphoreType.DMA((WEIGHT_SLOTS,)),
            pltpu.SemaphoreType.DMA((SEND_SLOTS,)),
            pltpu.SemaphoreType.DMA((SEND_SLOTS,)),
            pltpu.SemaphoreType.DMA((chunks * S,)),
            pltpu.SemaphoreType.DMA,
            pltpu.SemaphoreType.DMA,
            pltpu.SemaphoreType.DMA((max(stages, 1),)),
            pltpu.SemaphoreType.DMA((max(stages, 1),)),
            pltpu.SemaphoreType.DMA,
            pltpu.SemaphoreType.DMA,
            pltpu.SemaphoreType.DMA,
            pltpu.SemaphoreType.DMA,
        ],
        compiler_params=pltpu.CompilerParams(
            collective_id=0, has_side_effects=True, vmem_limit_bytes=60 * 2**20
        ),
    )(query_weight, sign_input.reshape(ib, 1, INNER), sign_output.reshape(ob, 1, INNER), clip_level, calibration)

    result = result.reshape(n, cal_rows // C, ob, pr)
    return result.transpose(1, 2, 0, 3).reshape(cal_rows // C, rows_local)


def solution(mesh):
    placed = (
        P(("layer", "row"), "col"),
        P(("layer", "col")),
        P(("layer", "row")),
        P(("layer", "row"), "col"),
        P(("layer", "row"), "col"),
    )
    return jax.shard_map(
        shards, mesh=mesh, in_specs=placed, out_specs=P(("layer", "col"), "row"), check_vma=False
    )
```

```python
import functools

import jax
import jax.numpy as jnp
from jax import lax
from jax.experimental import pallas as pl
from jax.experimental.pallas import tpu as pltpu
from jax.sharding import PartitionSpec as P

INNER = 1024
D = 16384
BLK = 128
LEVEL_UNIT = 512
GROUP = 256
SEND_SLOTS = 3
WEIGHT_SLOTS = 3
MESH = pl.DeviceIdType.MESH


def bits_of(size):
    bits = []
    while size > 1:
        size //= 2
        bits.append(size)
    return bits


def flip(at, bit):
    return at + bit * (1 - 2 * lax.rem(at // bit, 2))


def exclusive_or(a, b, size):
    total = 0
    for bit in bits_of(size):
        total = total + bit * lax.rem(a // bit + b // bit, 2)
    return total


def sylvester(size):
    x = lax.broadcasted_iota(jnp.int32, (size, size), 0) & lax.broadcasted_iota(jnp.int32, (size, size), 1)
    x = x ^ (x >> 4)
    x = x ^ (x >> 2)
    x = x ^ (x >> 1)
    return (1 - 2 * (x & 1)).astype(jnp.float32)


def butterfly(values):
    values = list(values)
    half = 1
    while half < len(values):
        for at in range(len(values)):
            if not at & half:
                low, high = values[at], values[at + half]
                values[at], values[at + half] = low + high, low - high
        half *= 2
    return values


def kernel(
    R, C, w_ref, si_ref, so_ref, level_ref, cal_ref, recv_ref, out_ref,
    kout, skin, kin, wbuf, right, sbuf, rbuf, mix, clip, acc, accb, perm, calv, levv, levb, lim, ostage,
    wsem, ssem, own_sem, rsem, usem, cal_own, cal_send, cal_recv, lev_send, lev_recv, out_send, out_recv,
):
    layer, r, c = lax.axis_index("layer"), lax.axis_index("row"), lax.axis_index("col")
    n = R * C
    me = r * C + c
    units, _, ob, ds, wide = recv_ref.shape
    ib = wide // BLK
    chunks = INNER // BLK
    S = units // chunks
    pr = S * ds
    ao, ai = R * ob, C * ib
    groups = INNER // BLK
    blocks = ob * ib
    lev_cols = level_ref.shape[1]
    row_bits, col_bits = bits_of(R), bits_of(C)
    stages = len(row_bits) + len(col_bits)

    def peer(i):
        pr_, pc_ = exclusive_or(r, i // C, R), exclusive_or(c, lax.rem(i, C), C)
        return (layer, pr_, pc_), pr_ * C + pc_

    def w_copy(q):
        block, slot = lax.rem(q, blocks), lax.rem(q, WEIGHT_SLOTS)
        rows = pl.ds(pl.multiple_of((block // ib) * INNER, INNER), INNER)
        cols = pl.ds(pl.multiple_of(lax.rem(block, ib) * INNER, INNER), INNER)
        return pltpu.make_async_copy(w_ref.at[rows, cols], wbuf.at[slot], wsem.at[slot])

    def cal_slot(rr, cc):
        slot, weight = 0, 1
        for bit in row_bits:
            slot = slot + weight * lax.rem(r // bit + rr // bit, 2)
            weight *= 2
        for bit in col_bits:
            slot = slot + weight * lax.rem(c // bit + cc // bit, 2)
            weight *= 2
        return slot

    def cal_copy(stage):
        size = 2**stage
        if stage < len(row_bits):
            target = (layer, flip(r, row_bits[stage]), c)
        else:
            target = (layer, r, flip(c, col_bits[stage - len(row_bits)]))
        return pltpu.make_async_remote_copy(
            src_ref=cal_ref if stage == 0 else calv.at[pl.ds(0, size)],
            dst_ref=calv.at[1] if stage == 0 else calv.at[pl.ds(size, size)],
            send_sem=cal_send.at[stage],
            recv_sem=cal_recv.at[stage],
            device_id=target,
            device_id_type=MESH,
        )

    cal_own_copy = pltpu.make_async_copy(cal_ref, calv.at[0], cal_own)

    def cal_advance(stage):
        if stage >= stages:
            return
        if stage == 0:
            cal_own_copy.wait()
        cal_copy(stage).wait_recv()
        if stage + 1 < stages:
            cal_copy(stage + 1).start()

    barrier = pltpu.get_barrier_semaphore()

    @pl.loop(1, n)
    def _(i):
        target, _ = peer(i)
        pl.semaphore_signal(barrier, inc=1, device_id=target, device_id_type=MESH)

    cal_own_copy.start()
    for q in range(WEIGHT_SLOTS - 1):
        w_copy(q).start()
    pl.semaphore_wait(barrier, n - 1)

    if stages:
        cal_copy(0).start()
    pltpu.make_async_copy(level_ref, levv.at[me], lev_recv).start()

    @pl.loop(1, n)
    def _(i):
        target, _ = peer(i)
        pltpu.make_async_remote_copy(
            src_ref=level_ref, dst_ref=levv.at[me], send_sem=lev_send, recv_sem=lev_recv,
            device_id=target, device_id_type=MESH,
        ).start()

    table = sylvester(BLK)
    table_b = table.astype(jnp.bfloat16)
    diagonal = lax.broadcasted_iota(jnp.int32, (BLK, BLK), 0) == lax.broadcasted_iota(jnp.int32, (BLK, BLK), 1)

    def static_sign(a, b):
        return 1.0 - 2.0 * (bin(a & b).count("1") & 1)

    @pl.loop(0, ib)
    def _(k):
        for g in range(groups):
            signs = si_ref[k, :, g * BLK : (g + 1) * BLK].astype(jnp.float32)
            scaled = jnp.where(diagonal, signs, 0.0).astype(jnp.bfloat16)
            skin[k, g * BLK : (g + 1) * BLK, :] = jnp.dot(
                scaled, table_b, preferred_element_type=jnp.float32
            ).astype(jnp.bfloat16)

    @pl.loop(0, ob)
    def _(j):
        for g in range(groups):
            signs = so_ref[j, :, g * BLK : (g + 1) * BLK].astype(jnp.float32)
            plus = (table * signs).astype(jnp.bfloat16)
            minus = (table * -signs).astype(jnp.bfloat16)
            for h in range(groups):
                kout[j, h * BLK : (h + 1) * BLK, g * BLK : (g + 1) * BLK] = plus if static_sign(g, h) > 0 else minus

    def inner(t, slot):
        for g in range(groups):
            parity = 0
            for bit in bits_of(groups):
                if g & bit:
                    parity = parity + lax.rem(t // bit, 2)
            sign = (1 - 2 * lax.rem(parity + 0 * t, 2)).astype(jnp.float32)
            for k in range(ib):
                rows = slice(g * BLK, (g + 1) * BLK)
                kin[k, rows, :] = (skin[k, rows, :].astype(jnp.float32) * sign).astype(jnp.bfloat16)

        @pl.loop(0, ob)
        def _(j):
            @pl.loop(0, ib)
            def _(k):
                q = (t * ob + j) * ib + k
                w_copy(q).wait()

                @pl.when(q + WEIGHT_SLOTS - 1 < chunks * blocks)
                def _():
                    w_copy(q + WEIGHT_SLOTS - 1).start()

                wslot = lax.rem(q, WEIGHT_SLOTS)

                @pl.loop(0, INNER // GROUP)
                def _(m):
                    rows = pl.ds(pl.multiple_of(m * GROUP, GROUP), GROUP)
                    cols = pl.ds(pl.multiple_of(k * BLK, BLK), BLK)
                    right[rows, cols] = jnp.dot(
                        wbuf[wslot, rows, :], kin[k], preferred_element_type=jnp.float32
                    ).astype(jnp.bfloat16)

            @pl.loop(0, INNER // GROUP)
            def _(m):
                rows = pl.ds(pl.multiple_of(m * GROUP, GROUP), GROUP)
                both = jnp.dot(kout[j, rows, :], right[...], preferred_element_type=jnp.float32)
                per = GROUP // pr
                sbuf[slot, pl.ds(m * per, per), :, j] = both.reshape(per, S, ds, wide).astype(jnp.bfloat16)

    def send(t, slot):
        @pl.loop(0, S)
        def _(s):
            u = t * S + s
            pltpu.make_async_copy(sbuf.at[slot, me, s], recv_ref.at[u, me], own_sem.at[slot]).start()

            @pl.loop(1, n)
            def _(i):
                target, place = peer(n - i)
                pltpu.make_async_remote_copy(
                    src_ref=sbuf.at[slot, place, s], dst_ref=recv_ref.at[u, me],
                    send_sem=ssem.at[slot], recv_sem=rsem.at[u],
                    device_id=target, device_id_type=MESH,
                ).start()

    def wait_send(slot):
        sent = sbuf.at[slot, pl.ds(0, n - 1)]
        pltpu.make_async_copy(sent, sent, ssem.at[slot]).wait()

    def wait_own(slot):
        own = sbuf.at[slot, me]
        pltpu.make_async_copy(own, own, own_sem.at[slot]).wait()

    d_block = me * pr // BLK
    d_blocks = INNER // BLK

    def read_levels():
        pltpu.make_async_copy(levv, levv, lev_recv).wait()
        level = levv[...].astype(jnp.float32).reshape(n * ob, d_blocks, lev_cols)
        line = lax.broadcasted_iota(jnp.int32, level.shape, 1)
        level = jnp.sum(jnp.where(line == d_block, level, 0.0), axis=1, keepdims=True)
        level = jnp.broadcast_to(level, (n * ob, d_blocks, lev_cols)).reshape(n * ob * d_blocks, lev_cols)
        levb[...] = level.astype(jnp.bfloat16)

    def outer(t):
        lane = lax.broadcasted_iota(jnp.int32, (lev_cols, wide), 1)
        line = lax.broadcasted_iota(jnp.int32, (lev_cols, wide), 0)
        pick = jnp.where(line == (lane >> 7) * d_blocks + t, float(D // LEVEL_UNIT), 0.0).astype(jnp.bfloat16)
        lim[...] = jnp.dot(levb[...], pick, preferred_element_type=jnp.float32).reshape(lim.shape)

        @pl.loop(0, S)
        def _(s):
            u = t * S + s
            arrived = recv_ref.at[u, pl.ds(0, n - 1)]
            pltpu.make_async_copy(arrived, arrived, rsem.at[u]).wait()
            fetch = pltpu.make_async_copy(recv_ref.at[u], rbuf, usem)
            fetch.start()
            fetch.wait()

            @pl.loop(0, ai)
            def _(i):
                cc, k = i // ib, lax.rem(i, ib)
                cols = pl.ds(pl.multiple_of(k * BLK, BLK), BLK)
                mixed = butterfly(
                    rbuf[rr * C + cc, j, :, cols].astype(jnp.float32) for rr in range(R) for j in range(ob)
                )
                for o in range(ao):
                    mix[i, o] = mixed[o]

            @pl.loop(0, ao)
            def _(o):
                rr, j = o // ob, lax.rem(o, ob)
                mixed = butterfly(mix[i, o] for i in range(ai))
                for i in range(ai):
                    cc, k = i // ib, i % ib
                    limit = lim[(rr * C + cc) * ob + j, :, k * BLK : (k + 1) * BLK]
                    value = mixed[i].reshape(ds // d_blocks, d_blocks, BLK)
                    value = jnp.minimum(jnp.maximum(value, -limit), limit)
                    clip[i, o] = value.reshape(ds, BLK).astype(jnp.bfloat16)

            total = None
            for i in range(ai):
                cc, k = i // ib, i % ib
                cols = pl.ds(pl.multiple_of(k * INNER + t * BLK, BLK), BLK)
                cal = jnp.concatenate([calv[cal_slot(rr, cc), :, cols] for rr in range(R)], axis=0)
                term = lax.dot_general(
                    cal, clip[i].reshape(ao * ds, BLK), (((1,), (1,)), ((), ())), preferred_element_type=jnp.float32
                )
                total = term if total is None else total + term
            acc[s] += total

    spot = lax.broadcasted_iota(jnp.int32, perm.shape[1:], 0)
    lane = lax.broadcasted_iota(jnp.int32, perm.shape[1:], 1)
    shift = pr.bit_length() - 1
    step = ds.bit_length() - 1
    for q in range(R):
        for s in range(S):
            wanted = (q * ob + (lane >> shift)) * ds + (lane & (ds - 1))
            hit = (spot == wanted) & (((lane & (pr - 1)) >> step) == s)
            perm[q * S + s] = jnp.where(hit, 1.0, 0.0).astype(jnp.bfloat16)
    acc[...] = jnp.zeros_like(acc)

    @pl.loop(0, chunks + SEND_SLOTS)
    def _(i):
        slot = lax.rem(i, SEND_SLOTS)

        @pl.when(i >= SEND_SLOTS)
        def _():
            wait_own(slot)

        @pl.when(i < chunks)
        def _():
            @pl.when(i >= SEND_SLOTS)
            def _():
                wait_send(slot)

            inner(i, slot)
            send(i, slot)

        for at in range(SEND_SLOTS + 1):
            @pl.when(i == at)
            def _():
                cal_advance(at)
                if at == SEND_SLOTS:
                    for later in range(at + 1, stages):
                        cal_advance(later)
                    read_levels()

        @pl.when(i >= SEND_SLOTS)
        def _():
            outer(i - SEND_SLOTS)

    accb[...] = (acc[...] * (1.0 / D)).astype(jnp.bfloat16)
    rows_each = ostage.shape[1]

    @pl.loop(0, R)
    def _(q):
        total = None
        for s in range(S):
            term = jnp.dot(accb[s], perm[q * S + s], preferred_element_type=jnp.float32)
            total = term if total is None else total + term
        for cc in range(C):
            ostage[q * C + cc] = total[cc * rows_each : (cc + 1) * rows_each].astype(jnp.bfloat16)

    pltpu.make_async_copy(ostage.at[me], out_ref.at[me], out_recv).start()

    @pl.loop(1, n)
    def _(i):
        target, place = peer(n - i)
        pltpu.make_async_remote_copy(
            src_ref=ostage.at[place], dst_ref=out_ref.at[me], send_sem=out_send, recv_sem=out_recv,
            device_id=target, device_id_type=MESH,
        ).start()

    for t in range(chunks - SEND_SLOTS, chunks):
        wait_send(t % SEND_SLOTS)
    for stage in range(stages):
        cal_copy(stage).wait_send()
    sent = levv.at[pl.ds(0, n - 1)]
    pltpu.make_async_copy(sent, sent, lev_send).wait()
    pltpu.make_async_copy(out_ref, out_ref, out_recv).wait()
    sent = ostage.at[pl.ds(0, n - 1)]
    pltpu.make_async_copy(sent, sent, out_send).wait()


def shards(query_weight, sign_input, sign_output, clip_level, calibration):
    rows_local, cols_local = query_weight.shape
    R, C = lax.axis_size("row"), lax.axis_size("col")
    n = R * C
    ob, ib = rows_local // INNER, cols_local // INNER
    pr = INNER // n
    ds = min(16, pr)
    S = pr // ds
    chunks = INNER // BLK
    cal_local = calibration.shape[0]
    cal_rows = R * cal_local
    ao, ai = R * ob, C * ib
    wide = ib * BLK
    stages = len(bits_of(R)) + len(bits_of(C))
    bf16, f32 = jnp.bfloat16, jnp.float32

    _, result = pl.pallas_call(
        functools.partial(kernel, R, C),
        in_specs=[
            pl.BlockSpec(memory_space=pl.ANY),
            pl.BlockSpec(memory_space=pltpu.VMEM),
            pl.BlockSpec(memory_space=pltpu.VMEM),
            pl.BlockSpec(memory_space=pl.ANY),
            pl.BlockSpec(memory_space=pl.ANY),
        ],
        out_specs=[pl.BlockSpec(memory_space=pl.ANY)] * 2,
        out_shape=[
            jax.ShapeDtypeStruct((chunks * S, n, ob, ds, wide), bf16),
            jax.ShapeDtypeStruct((n, cal_rows // C, ob * pr), bf16),
        ],
        scratch_shapes=[
            pltpu.VMEM((ob, INNER, INNER), bf16),
            pltpu.VMEM((ib, INNER, BLK), bf16),
            pltpu.VMEM((ib, INNER, BLK), bf16),
            pltpu.VMEM((WEIGHT_SLOTS, INNER, INNER), bf16),
            pltpu.VMEM((INNER, wide), bf16),
            pltpu.VMEM((SEND_SLOTS, n, S, ob, ds, wide), bf16),
            pltpu.VMEM((n, ob, ds, wide), bf16),
            pltpu.VMEM((ai, ao, ds, BLK), f32),
            pltpu.VMEM((ai, ao, ds, BLK), bf16),
            pltpu.VMEM((S, cal_rows, ao * ds), f32),
            pltpu.VMEM((S, cal_rows, ao * ds), bf16),
            pltpu.VMEM((R * S, ao * ds, ob * pr), bf16),
            pltpu.VMEM((n, cal_local, cols_local), bf16),
            pltpu.VMEM((n,) + clip_level.shape, jnp.int32),
            pltpu.VMEM((n * clip_level.shape[0], clip_level.shape[1]), bf16),
            pltpu.VMEM((n * ob, INNER // BLK, wide), f32),
            pltpu.VMEM((n, cal_rows // C, ob * pr), bf16),
            pltpu.SemaphoreType.DMA((WEIGHT_SLOTS,)),
            pltpu.SemaphoreType.DMA((SEND_SLOTS,)),
            pltpu.SemaphoreType.DMA((SEND_SLOTS,)),
            pltpu.SemaphoreType.DMA((chunks * S,)),
            pltpu.SemaphoreType.DMA,
            pltpu.SemaphoreType.DMA,
            pltpu.SemaphoreType.DMA((max(stages, 1),)),
            pltpu.SemaphoreType.DMA((max(stages, 1),)),
            pltpu.SemaphoreType.DMA,
            pltpu.SemaphoreType.DMA,
            pltpu.SemaphoreType.DMA,
            pltpu.SemaphoreType.DMA,
        ],
        compiler_params=pltpu.CompilerParams(
            collective_id=0, has_side_effects=True, vmem_limit_bytes=60 * 2**20
        ),
    )(query_weight, sign_input.reshape(ib, 1, INNER), sign_output.reshape(ob, 1, INNER), clip_level, calibration)

    result = result.reshape(n, cal_rows // C, ob, pr)
    return result.transpose(1, 2, 0, 3).reshape(cal_rows // C, rows_local)


def solution(mesh):
    placed = (
        P(("layer", "row"), "col"),
        P(("layer", "col")),
        P(("layer", "row")),
        P(("layer", "row"), "col"),
        P(("layer", "row"), "col"),
    )
    return jax.shard_map(
        shards, mesh=mesh, in_specs=placed, out_specs=P(("layer", "col"), "row"), check_vma=False
    )
```

```python
import functools

import jax
import jax.numpy as jnp
from jax import lax
from jax.experimental import pallas as pl
from jax.experimental.pallas import tpu as pltpu
from jax.sharding import PartitionSpec as P

INNER = 1024
D = 16384
BLK = 128
LEVEL_UNIT = 512
GROUP = 256
SEND_SLOTS = 3
WEIGHT_SLOTS = 3
MESH = pl.DeviceIdType.MESH


def bits_of(size):
    bits = []
    while size > 1:
        size //= 2
        bits.append(size)
    return bits


def mixed_order(n, i):
    return n // 2 * lax.rem(i, 2) + i // 2


def flip(at, bit):
    return at + bit * (1 - 2 * lax.rem(at // bit, 2))


def exclusive_or(a, b, size):
    total = 0
    for bit in bits_of(size):
        total = total + bit * lax.rem(a // bit + b // bit, 2)
    return total


def sylvester(size):
    x = lax.broadcasted_iota(jnp.int32, (size, size), 0) & lax.broadcasted_iota(jnp.int32, (size, size), 1)
    x = x ^ (x >> 4)
    x = x ^ (x >> 2)
    x = x ^ (x >> 1)
    return (1 - 2 * (x & 1)).astype(jnp.float32)


def butterfly(values):
    values = list(values)
    half = 1
    while half < len(values):
        for at in range(len(values)):
            if not at & half:
                low, high = values[at], values[at + half]
                values[at], values[at + half] = low + high, low - high
        half *= 2
    return values


def kernel(
    R, C, w_ref, si_ref, so_ref, level_ref, cal_ref, recv_ref, out_ref,
    kout, skin, kin, wbuf, right, sbuf, rbuf, mix, clip, acc, accb, perm, calv, levv, levb, lim, ostage,
    wsem, ssem, own_sem, rsem, usem, cal_own, cal_send, cal_recv, lev_send, lev_recv, out_send, out_recv,
):
    layer, r, c = lax.axis_index("layer"), lax.axis_index("row"), lax.axis_index("col")
    n = R * C
    me = r * C + c
    units, _, ob, ds, wide = recv_ref.shape
    ib = wide // BLK
    chunks = INNER // BLK
    S = units // chunks
    pr = S * ds
    ao, ai = R * ob, C * ib
    groups = INNER // BLK
    blocks = ob * ib
    lev_cols = level_ref.shape[1]
    row_bits, col_bits = bits_of(R), bits_of(C)
    stages = len(row_bits) + len(col_bits)

    def peer(i):
        pr_, pc_ = exclusive_or(r, i // C, R), exclusive_or(c, lax.rem(i, C), C)
        return (layer, pr_, pc_), pr_ * C + pc_

    def w_copy(q):
        block, slot = lax.rem(q, blocks), lax.rem(q, WEIGHT_SLOTS)
        rows = pl.ds(pl.multiple_of((block // ib) * INNER, INNER), INNER)
        cols = pl.ds(pl.multiple_of(lax.rem(block, ib) * INNER, INNER), INNER)
        return pltpu.make_async_copy(w_ref.at[rows, cols], wbuf.at[slot], wsem.at[slot])

    def cal_slot(rr, cc):
        slot, weight = 0, 1
        for bit in row_bits:
            slot = slot + weight * lax.rem(r // bit + rr // bit, 2)
            weight *= 2
        for bit in col_bits:
            slot = slot + weight * lax.rem(c // bit + cc // bit, 2)
            weight *= 2
        return slot

    def cal_copy(stage):
        size = 2**stage
        if stage < len(row_bits):
            target = (layer, flip(r, row_bits[stage]), c)
        else:
            target = (layer, r, flip(c, col_bits[stage - len(row_bits)]))
        return pltpu.make_async_remote_copy(
            src_ref=cal_ref if stage == 0 else calv.at[pl.ds(0, size)],
            dst_ref=calv.at[1] if stage == 0 else calv.at[pl.ds(size, size)],
            send_sem=cal_send.at[stage],
            recv_sem=cal_recv.at[stage],
            device_id=target,
            device_id_type=MESH,
        )

    cal_own_copy = pltpu.make_async_copy(cal_ref, calv.at[0], cal_own)

    def cal_advance(stage):
        if stage >= stages:
            return
        if stage == 0:
            cal_own_copy.wait()
        cal_copy(stage).wait_recv()
        if stage + 1 < stages:
            cal_copy(stage + 1).start()

    barrier = pltpu.get_barrier_semaphore()

    @pl.loop(1, n)
    def _(i):
        target, _ = peer(i)
        pl.semaphore_signal(barrier, inc=1, device_id=target, device_id_type=MESH)

    cal_own_copy.start()
    for q in range(WEIGHT_SLOTS - 1):
        w_copy(q).start()
    pl.semaphore_wait(barrier, n - 1)

    if stages:
        cal_copy(0).start()
    pltpu.make_async_copy(level_ref, levv.at[me], lev_recv).start()

    @pl.loop(1, n)
    def _(i):
        target, _ = peer(i)
        pltpu.make_async_remote_copy(
            src_ref=level_ref, dst_ref=levv.at[me], send_sem=lev_send, recv_sem=lev_recv,
            device_id=target, device_id_type=MESH,
        ).start()

    table = sylvester(BLK)
    table_b = table.astype(jnp.bfloat16)
    diagonal = lax.broadcasted_iota(jnp.int32, (BLK, BLK), 0) == lax.broadcasted_iota(jnp.int32, (BLK, BLK), 1)

    def static_sign(a, b):
        return 1.0 - 2.0 * (bin(a & b).count("1") & 1)

    @pl.loop(0, ib)
    def _(k):
        for g in range(groups):
            signs = si_ref[k, :, g * BLK : (g + 1) * BLK].astype(jnp.float32)
            scaled = jnp.where(diagonal, signs, 0.0).astype(jnp.bfloat16)
            skin[k, g * BLK : (g + 1) * BLK, :] = jnp.dot(
                scaled, table_b, preferred_element_type=jnp.float32
            ).astype(jnp.bfloat16)

    @pl.loop(0, ob)
    def _(j):
        for g in range(groups):
            signs = so_ref[j, :, g * BLK : (g + 1) * BLK].astype(jnp.float32)
            plus = (table * signs).astype(jnp.bfloat16)
            minus = (table * -signs).astype(jnp.bfloat16)
            for h in range(groups):
                kout[j, h * BLK : (h + 1) * BLK, g * BLK : (g + 1) * BLK] = plus if static_sign(g, h) > 0 else minus

    def inner(t, slot):
        for g in range(groups):
            parity = 0
            for bit in bits_of(groups):
                if g & bit:
                    parity = parity + lax.rem(t // bit, 2)
            sign = (1 - 2 * lax.rem(parity + 0 * t, 2)).astype(jnp.float32)
            for k in range(ib):
                rows = slice(g * BLK, (g + 1) * BLK)
                kin[k, rows, :] = (skin[k, rows, :].astype(jnp.float32) * sign).astype(jnp.bfloat16)

        @pl.loop(0, ob)
        def _(j):
            @pl.loop(0, ib)
            def _(k):
                q = (t * ob + j) * ib + k
                w_copy(q).wait()

                @pl.when(q + WEIGHT_SLOTS - 1 < chunks * blocks)
                def _():
                    w_copy(q + WEIGHT_SLOTS - 1).start()

                wslot = lax.rem(q, WEIGHT_SLOTS)

                @pl.loop(0, INNER // GROUP)
                def _(m):
                    rows = pl.ds(pl.multiple_of(m * GROUP, GROUP), GROUP)
                    cols = pl.ds(pl.multiple_of(k * BLK, BLK), BLK)
                    right[rows, cols] = jnp.dot(
                        wbuf[wslot, rows, :], kin[k], preferred_element_type=jnp.float32
                    ).astype(jnp.bfloat16)

            @pl.loop(0, INNER // GROUP)
            def _(m):
                rows = pl.ds(pl.multiple_of(m * GROUP, GROUP), GROUP)
                both = jnp.dot(kout[j, rows, :], right[...], preferred_element_type=jnp.float32)
                per = GROUP // pr
                sbuf[slot, pl.ds(m * per, per), :, j] = both.reshape(per, S, ds, wide).astype(jnp.bfloat16)

    def send(t, slot):
        @pl.loop(0, S)
        def _(s):
            u = t * S + s
            pltpu.make_async_copy(sbuf.at[slot, me, s], recv_ref.at[u, me], own_sem.at[slot]).start()

            @pl.loop(1, n)
            def _(i):
                target, place = peer(mixed_order(n, i))
                pltpu.make_async_remote_copy(
                    src_ref=sbuf.at[slot, place, s], dst_ref=recv_ref.at[u, me],
                    send_sem=ssem.at[slot], recv_sem=rsem.at[u],
                    device_id=target, device_id_type=MESH,
                ).start()

    def wait_send(slot):
        sent = sbuf.at[slot, pl.ds(0, n - 1)]
        pltpu.make_async_copy(sent, sent, ssem.at[slot]).wait()

    def wait_own(slot):
        own = sbuf.at[slot, me]
        pltpu.make_async_copy(own, own, own_sem.at[slot]).wait()

    d_block = me * pr // BLK
    d_blocks = INNER // BLK

    def read_levels():
        pltpu.make_async_copy(levv, levv, lev_recv).wait()
        level = levv[...].astype(jnp.float32).reshape(n * ob, d_blocks, lev_cols)
        line = lax.broadcasted_iota(jnp.int32, level.shape, 1)
        level = jnp.sum(jnp.where(line == d_block, level, 0.0), axis=1, keepdims=True)
        level = jnp.broadcast_to(level, (n * ob, d_blocks, lev_cols)).reshape(n * ob * d_blocks, lev_cols)
        levb[...] = level.astype(jnp.bfloat16)

    def outer(t):
        lane = lax.broadcasted_iota(jnp.int32, (lev_cols, wide), 1)
        line = lax.broadcasted_iota(jnp.int32, (lev_cols, wide), 0)
        pick = jnp.where(line == (lane >> 7) * d_blocks + t, float(D // LEVEL_UNIT), 0.0).astype(jnp.bfloat16)
        lim[...] = jnp.dot(levb[...], pick, preferred_element_type=jnp.float32).reshape(lim.shape)

        @pl.loop(0, S)
        def _(s):
            u = t * S + s
            arrived = recv_ref.at[u, pl.ds(0, n - 1)]
            pltpu.make_async_copy(arrived, arrived, rsem.at[u]).wait()
            fetch = pltpu.make_async_copy(recv_ref.at[u], rbuf, usem)
            fetch.start()
            fetch.wait()

            @pl.loop(0, ai)
            def _(i):
                cc, k = i // ib, lax.rem(i, ib)
                cols = pl.ds(pl.multiple_of(k * BLK, BLK), BLK)
                mixed = butterfly(
                    rbuf[rr * C + cc, j, :, cols].astype(jnp.float32) for rr in range(R) for j in range(ob)
                )
                for o in range(ao):
                    mix[i, o] = mixed[o]

            @pl.loop(0, ao)
            def _(o):
                rr, j = o // ob, lax.rem(o, ob)
                mixed = butterfly(mix[i, o] for i in range(ai))
                for i in range(ai):
                    cc, k = i // ib, i % ib
                    limit = lim[(rr * C + cc) * ob + j, :, k * BLK : (k + 1) * BLK]
                    value = mixed[i].reshape(ds // d_blocks, d_blocks, BLK)
                    value = jnp.minimum(jnp.maximum(value, -limit), limit)
                    clip[i, o] = value.reshape(ds, BLK).astype(jnp.bfloat16)

            total = None
            for i in range(ai):
                cc, k = i // ib, i % ib
                cols = pl.ds(pl.multiple_of(k * INNER + t * BLK, BLK), BLK)
                cal = jnp.concatenate([calv[cal_slot(rr, cc), :, cols] for rr in range(R)], axis=0)
                term = lax.dot_general(
                    cal, clip[i].reshape(ao * ds, BLK), (((1,), (1,)), ((), ())), preferred_element_type=jnp.float32
                )
                total = term if total is None else total + term
            acc[s] += total

    spot = lax.broadcasted_iota(jnp.int32, perm.shape[1:], 0)
    lane = lax.broadcasted_iota(jnp.int32, perm.shape[1:], 1)
    shift = pr.bit_length() - 1
    step = ds.bit_length() - 1
    for q in range(R):
        for s in range(S):
            wanted = (q * ob + (lane >> shift)) * ds + (lane & (ds - 1))
            hit = (spot == wanted) & (((lane & (pr - 1)) >> step) == s)
            perm[q * S + s] = jnp.where(hit, 1.0, 0.0).astype(jnp.bfloat16)
    acc[...] = jnp.zeros_like(acc)

    @pl.loop(0, chunks + SEND_SLOTS)
    def _(i):
        slot = lax.rem(i, SEND_SLOTS)

        @pl.when(i >= SEND_SLOTS)
        def _():
            wait_own(slot)

        @pl.when(i < chunks)
        def _():
            @pl.when(i >= SEND_SLOTS)
            def _():
                wait_send(slot)

            inner(i, slot)
            send(i, slot)

        for at in range(SEND_SLOTS + 1):
            @pl.when(i == at)
            def _():
                cal_advance(at)
                if at == SEND_SLOTS:
                    for later in range(at + 1, stages):
                        cal_advance(later)
                    read_levels()

        @pl.when(i >= SEND_SLOTS)
        def _():
            outer(i - SEND_SLOTS)

    accb[...] = (acc[...] * (1.0 / D)).astype(jnp.bfloat16)
    rows_each = ostage.shape[1]

    @pl.loop(0, R)
    def _(q):
        total = None
        for s in range(S):
            term = jnp.dot(accb[s], perm[q * S + s], preferred_element_type=jnp.float32)
            total = term if total is None else total + term
        for cc in range(C):
            ostage[q * C + cc] = total[cc * rows_each : (cc + 1) * rows_each].astype(jnp.bfloat16)

    pltpu.make_async_copy(ostage.at[me], out_ref.at[me], out_recv).start()

    @pl.loop(1, n)
    def _(i):
        target, place = peer(n - i)
        pltpu.make_async_remote_copy(
            src_ref=ostage.at[place], dst_ref=out_ref.at[me], send_sem=out_send, recv_sem=out_recv,
            device_id=target, device_id_type=MESH,
        ).start()

    for t in range(chunks - SEND_SLOTS, chunks):
        wait_send(t % SEND_SLOTS)
    for stage in range(stages):
        cal_copy(stage).wait_send()
    sent = levv.at[pl.ds(0, n - 1)]
    pltpu.make_async_copy(sent, sent, lev_send).wait()
    pltpu.make_async_copy(out_ref, out_ref, out_recv).wait()
    sent = ostage.at[pl.ds(0, n - 1)]
    pltpu.make_async_copy(sent, sent, out_send).wait()


def shards(query_weight, sign_input, sign_output, clip_level, calibration):
    rows_local, cols_local = query_weight.shape
    R, C = lax.axis_size("row"), lax.axis_size("col")
    n = R * C
    ob, ib = rows_local // INNER, cols_local // INNER
    pr = INNER // n
    ds = min(16, pr)
    S = pr // ds
    chunks = INNER // BLK
    cal_local = calibration.shape[0]
    cal_rows = R * cal_local
    ao, ai = R * ob, C * ib
    wide = ib * BLK
    stages = len(bits_of(R)) + len(bits_of(C))
    bf16, f32 = jnp.bfloat16, jnp.float32

    _, result = pl.pallas_call(
        functools.partial(kernel, R, C),
        in_specs=[
            pl.BlockSpec(memory_space=pl.ANY),
            pl.BlockSpec(memory_space=pltpu.VMEM),
            pl.BlockSpec(memory_space=pltpu.VMEM),
            pl.BlockSpec(memory_space=pl.ANY),
            pl.BlockSpec(memory_space=pl.ANY),
        ],
        out_specs=[pl.BlockSpec(memory_space=pl.ANY)] * 2,
        out_shape=[
            jax.ShapeDtypeStruct((chunks * S, n, ob, ds, wide), bf16),
            jax.ShapeDtypeStruct((n, cal_rows // C, ob * pr), bf16),
        ],
        scratch_shapes=[
            pltpu.VMEM((ob, INNER, INNER), bf16),
            pltpu.VMEM((ib, INNER, BLK), bf16),
            pltpu.VMEM((ib, INNER, BLK), bf16),
            pltpu.VMEM((WEIGHT_SLOTS, INNER, INNER), bf16),
            pltpu.VMEM((INNER, wide), bf16),
            pltpu.VMEM((SEND_SLOTS, n, S, ob, ds, wide), bf16),
            pltpu.VMEM((n, ob, ds, wide), bf16),
            pltpu.VMEM((ai, ao, ds, BLK), f32),
            pltpu.VMEM((ai, ao, ds, BLK), bf16),
            pltpu.VMEM((S, cal_rows, ao * ds), f32),
            pltpu.VMEM((S, cal_rows, ao * ds), bf16),
            pltpu.VMEM((R * S, ao * ds, ob * pr), bf16),
            pltpu.VMEM((n, cal_local, cols_local), bf16),
            pltpu.VMEM((n,) + clip_level.shape, jnp.int32),
            pltpu.VMEM((n * clip_level.shape[0], clip_level.shape[1]), bf16),
            pltpu.VMEM((n * ob, INNER // BLK, wide), f32),
            pltpu.VMEM((n, cal_rows // C, ob * pr), bf16),
            pltpu.SemaphoreType.DMA((WEIGHT_SLOTS,)),
            pltpu.SemaphoreType.DMA((SEND_SLOTS,)),
            pltpu.SemaphoreType.DMA((SEND_SLOTS,)),
            pltpu.SemaphoreType.DMA((chunks * S,)),
            pltpu.SemaphoreType.DMA,
            pltpu.SemaphoreType.DMA,
            pltpu.SemaphoreType.DMA((max(stages, 1),)),
            pltpu.SemaphoreType.DMA((max(stages, 1),)),
            pltpu.SemaphoreType.DMA,
            pltpu.SemaphoreType.DMA,
            pltpu.SemaphoreType.DMA,
            pltpu.SemaphoreType.DMA,
        ],
        compiler_params=pltpu.CompilerParams(
            collective_id=0, has_side_effects=True, vmem_limit_bytes=60 * 2**20
        ),
    )(query_weight, sign_input.reshape(ib, 1, INNER), sign_output.reshape(ob, 1, INNER), clip_level, calibration)

    result = result.reshape(n, cal_rows // C, ob, pr)
    return result.transpose(1, 2, 0, 3).reshape(cal_rows // C, rows_local)


def solution(mesh):
    placed = (
        P(("layer", "row"), "col"),
        P(("layer", "col")),
        P(("layer", "row")),
        P(("layer", "row"), "col"),
        P(("layer", "row"), "col"),
    )
    return jax.shard_map(
        shards, mesh=mesh, in_specs=placed, out_specs=P(("layer", "col"), "row"), check_vma=False
    )
```

```python
import functools

import jax
import jax.numpy as jnp
from jax import lax
from jax.experimental import pallas as pl
from jax.experimental.pallas import tpu as pltpu
from jax.sharding import PartitionSpec as P

INNER = 1024
D = 16384
BLK = 128
LEVEL_UNIT = 512
GROUP = 256
SEND_SLOTS = 3
WEIGHT_SLOTS = 3
MESH = pl.DeviceIdType.MESH


def bits_of(size):
    bits = []
    while size > 1:
        size //= 2
        bits.append(size)
    return bits


def mixed_order(n, i):
    return n // 2 * lax.rem(i, 2) + i // 2


def flip(at, bit):
    return at + bit * (1 - 2 * lax.rem(at // bit, 2))


def exclusive_or(a, b, size):
    total = 0
    for bit in bits_of(size):
        total = total + bit * lax.rem(a // bit + b // bit, 2)
    return total


def sylvester(size):
    x = lax.broadcasted_iota(jnp.int32, (size, size), 0) & lax.broadcasted_iota(jnp.int32, (size, size), 1)
    x = x ^ (x >> 4)
    x = x ^ (x >> 2)
    x = x ^ (x >> 1)
    return (1 - 2 * (x & 1)).astype(jnp.float32)


def butterfly(values):
    values = list(values)
    half = 1
    while half < len(values):
        for at in range(len(values)):
            if not at & half:
                low, high = values[at], values[at + half]
                values[at], values[at + half] = low + high, low - high
        half *= 2
    return values


def kernel(
    R, C, w_ref, si_hbm, so_hbm, level_ref, cal_ref, recv_ref, out_ref,
    si_ref, so_ref, kout, skin, kin, wbuf, right, sbuf, rbuf, mix, clip, acc, accb, perm, calv, levv, levb, lim, ostage,
    sign_sem, wsem, ssem, own_sem, rsem, usem, cal_own, cal_send, cal_recv, lev_send, lev_recv, out_send, out_recv,
):
    layer, r, c = lax.axis_index("layer"), lax.axis_index("row"), lax.axis_index("col")
    n = R * C
    me = r * C + c
    units, _, ob, ds, wide = recv_ref.shape
    ib = wide // BLK
    chunks = INNER // BLK
    S = units // chunks
    H = out_ref.shape[0]
    last = chunks - 1
    pr = S * ds
    ao, ai = R * ob, C * ib
    groups = INNER // BLK
    blocks = ob * ib
    lev_cols = level_ref.shape[1]
    row_bits, col_bits = bits_of(R), bits_of(C)
    stages = len(row_bits) + len(col_bits)

    def peer(i):
        pr_, pc_ = exclusive_or(r, i // C, R), exclusive_or(c, lax.rem(i, C), C)
        return (layer, pr_, pc_), pr_ * C + pc_

    def w_copy(q):
        block, slot = lax.rem(q, blocks), lax.rem(q, WEIGHT_SLOTS)
        rows = pl.ds(pl.multiple_of((block // ib) * INNER, INNER), INNER)
        cols = pl.ds(pl.multiple_of(lax.rem(block, ib) * INNER, INNER), INNER)
        return pltpu.make_async_copy(w_ref.at[rows, cols], wbuf.at[slot], wsem.at[slot])

    def cal_slot(rr, cc):
        slot, weight = 0, 1
        for bit in row_bits:
            slot = slot + weight * lax.rem(r // bit + rr // bit, 2)
            weight *= 2
        for bit in col_bits:
            slot = slot + weight * lax.rem(c // bit + cc // bit, 2)
            weight *= 2
        return slot

    def cal_copy(stage):
        size = 2**stage
        if stage < len(row_bits):
            target = (layer, flip(r, row_bits[stage]), c)
        else:
            target = (layer, r, flip(c, col_bits[stage - len(row_bits)]))
        return pltpu.make_async_remote_copy(
            src_ref=cal_ref if stage == 0 else calv.at[pl.ds(0, size)],
            dst_ref=calv.at[1] if stage == 0 else calv.at[pl.ds(size, size)],
            send_sem=cal_send.at[stage],
            recv_sem=cal_recv.at[stage],
            device_id=target,
            device_id_type=MESH,
        )

    cal_own_copy = pltpu.make_async_copy(cal_ref, calv.at[0], cal_own)

    def cal_advance(stage):
        if stage >= stages:
            return
        if stage == 0:
            cal_own_copy.wait()
        cal_copy(stage).wait_recv()
        if stage + 1 < stages:
            cal_copy(stage + 1).start()

    barrier = pltpu.get_barrier_semaphore()

    @pl.loop(1, n)
    def _(i):
        target, _ = peer(i)
        pl.semaphore_signal(barrier, inc=1, device_id=target, device_id_type=MESH)

    sign_copies = [
        pltpu.make_async_copy(si_hbm, si_ref, sign_sem.at[0]),
        pltpu.make_async_copy(so_hbm, so_ref, sign_sem.at[1]),
    ]
    for copy in sign_copies:
        copy.start()
    cal_own_copy.start()
    for q in range(WEIGHT_SLOTS - 1):
        w_copy(q).start()
    pl.semaphore_wait(barrier, n - 1)

    if stages:
        cal_copy(0).start()
    pltpu.make_async_copy(level_ref, levv.at[me], lev_recv).start()

    @pl.loop(1, n)
    def _(i):
        target, _ = peer(i)
        pltpu.make_async_remote_copy(
            src_ref=level_ref, dst_ref=levv.at[me], send_sem=lev_send, recv_sem=lev_recv,
            device_id=target, device_id_type=MESH,
        ).start()

    table = sylvester(BLK)
    table_b = table.astype(jnp.bfloat16)
    diagonal = lax.broadcasted_iota(jnp.int32, (BLK, BLK), 0) == lax.broadcasted_iota(jnp.int32, (BLK, BLK), 1)

    for copy in sign_copies:
        copy.wait()

    def static_sign(a, b):
        return 1.0 - 2.0 * (bin(a & b).count("1") & 1)

    @pl.loop(0, ib)
    def _(k):
        for g in range(groups):
            signs = si_ref[k, :, g * BLK : (g + 1) * BLK].astype(jnp.float32)
            scaled = jnp.where(diagonal, signs, 0.0).astype(jnp.bfloat16)
            skin[k, g * BLK : (g + 1) * BLK, :] = jnp.dot(
                scaled, table_b, preferred_element_type=jnp.float32
            ).astype(jnp.bfloat16)

    @pl.loop(0, ob)
    def _(j):
        for g in range(groups):
            signs = so_ref[j, :, g * BLK : (g + 1) * BLK].astype(jnp.float32)
            plus = (table * signs).astype(jnp.bfloat16)
            minus = (table * -signs).astype(jnp.bfloat16)
            for h in range(groups):
                kout[j, h * BLK : (h + 1) * BLK, g * BLK : (g + 1) * BLK] = plus if static_sign(g, h) > 0 else minus

    def inner(t, slot):
        for g in range(groups):
            parity = 0
            for bit in bits_of(groups):
                if g & bit:
                    parity = parity + lax.rem(t // bit, 2)
            sign = (1 - 2 * lax.rem(parity + 0 * t, 2)).astype(jnp.float32)
            for k in range(ib):
                rows = slice(g * BLK, (g + 1) * BLK)
                kin[k, rows, :] = (skin[k, rows, :].astype(jnp.float32) * sign).astype(jnp.bfloat16)

        @pl.loop(0, ob)
        def _(j):
            @pl.loop(0, ib)
            def _(k):
                q = (t * ob + j) * ib + k
                w_copy(q).wait()

                @pl.when(q + WEIGHT_SLOTS - 1 < chunks * blocks)
                def _():
                    w_copy(q + WEIGHT_SLOTS - 1).start()

                wslot = lax.rem(q, WEIGHT_SLOTS)

                @pl.loop(0, INNER // GROUP)
                def _(m):
                    rows = pl.ds(pl.multiple_of(m * GROUP, GROUP), GROUP)
                    cols = pl.ds(pl.multiple_of(k * BLK, BLK), BLK)
                    right[rows, cols] = jnp.dot(
                        wbuf[wslot, rows, :], kin[k], preferred_element_type=jnp.float32
                    ).astype(jnp.bfloat16)

            @pl.loop(0, INNER // GROUP)
            def _(m):
                rows = pl.ds(pl.multiple_of(m * GROUP, GROUP), GROUP)
                both = jnp.dot(kout[j, rows, :], right[...], preferred_element_type=jnp.float32)
                per = GROUP // pr
                sbuf[slot, pl.ds(m * per, per), :, j] = both.reshape(per, S, ds, wide).astype(jnp.bfloat16)

    def send(t, slot):
        @pl.loop(0, S)
        def _(s):
            u = t * S + s
            pltpu.make_async_copy(sbuf.at[slot, me, s], recv_ref.at[u, me], own_sem.at[slot]).start()

            @pl.loop(1, n)
            def _(i):
                target, place = peer(mixed_order(n, i))
                pltpu.make_async_remote_copy(
                    src_ref=sbuf.at[slot, place, s], dst_ref=recv_ref.at[u, me],
                    send_sem=ssem.at[slot], recv_sem=rsem.at[u],
                    device_id=target, device_id_type=MESH,
                ).start()

    def wait_send(slot):
        sent = sbuf.at[slot, pl.ds(0, n - 1)]
        pltpu.make_async_copy(sent, sent, ssem.at[slot]).wait()

    def wait_own(slot):
        own = sbuf.at[slot, me]
        pltpu.make_async_copy(own, own, own_sem.at[slot]).wait()

    d_block = me * pr // BLK
    d_blocks = INNER // BLK

    def read_levels():
        pltpu.make_async_copy(levv, levv, lev_recv).wait()
        level = levv[...].astype(jnp.float32).reshape(n * ob, d_blocks, lev_cols)
        line = lax.broadcasted_iota(jnp.int32, level.shape, 1)
        level = jnp.sum(jnp.where(line == d_block, level, 0.0), axis=1, keepdims=True)
        level = jnp.broadcast_to(level, (n * ob, d_blocks, lev_cols)).reshape(n * ob * d_blocks, lev_cols)
        levb[...] = level.astype(jnp.bfloat16)

    def finish(h):
        own_units = range(h * (S // H), (h + 1) * (S // H))
        rows_each = ostage.shape[2]
        for s in own_units:
            accb[s] = (acc[s] * (1.0 / D)).astype(jnp.bfloat16)

        @pl.loop(0, R)
        def _(q):
            total = None
            for s in own_units:
                term = jnp.dot(accb[s], perm[q * S + s], preferred_element_type=jnp.float32)
                total = term if total is None else total + term
            for cc in range(C):
                ostage[h, q * C + cc] = total[cc * rows_each : (cc + 1) * rows_each].astype(jnp.bfloat16)

    def send_out(h):
        pltpu.make_async_copy(ostage.at[h, me], out_ref.at[h, me], out_recv.at[h]).start()

        @pl.loop(1, n)
        def _(i):
            target, place = peer(n - i)
            pltpu.make_async_remote_copy(
                src_ref=ostage.at[h, place], dst_ref=out_ref.at[h, me],
                send_sem=out_send.at[h], recv_sem=out_recv.at[h],
                device_id=target, device_id_type=MESH,
            ).start()

    def outer(t):
        lane = lax.broadcasted_iota(jnp.int32, (lev_cols, wide), 1)
        line = lax.broadcasted_iota(jnp.int32, (lev_cols, wide), 0)
        pick = jnp.where(line == (lane >> 7) * d_blocks + t, float(D // LEVEL_UNIT), 0.0).astype(jnp.bfloat16)
        lim[...] = jnp.dot(levb[...], pick, preferred_element_type=jnp.float32).reshape(lim.shape)

        @pl.loop(0, S)
        def _(s):
            u = t * S + s
            final_unit = (t == last) & (s == S - 1)
            if H > 1:
                @pl.when(final_unit)
                def _():
                    finish(0)

            arrived = recv_ref.at[u, pl.ds(0, n - 1)]
            pltpu.make_async_copy(arrived, arrived, rsem.at[u]).wait()
            if H > 1:
                @pl.when(final_unit)
                def _():
                    send_out(0)

            fetch = pltpu.make_async_copy(recv_ref.at[u], rbuf, usem)
            fetch.start()
            fetch.wait()

            @pl.loop(0, ai)
            def _(i):
                cc, k = i // ib, lax.rem(i, ib)
                cols = pl.ds(pl.multiple_of(k * BLK, BLK), BLK)
                mixed = butterfly(
                    rbuf[rr * C + cc, j, :, cols].astype(jnp.float32) for rr in range(R) for j in range(ob)
                )
                for o in range(ao):
                    mix[i, o] = mixed[o]

            @pl.loop(0, ao)
            def _(o):
                rr, j = o // ob, lax.rem(o, ob)
                mixed = butterfly(mix[i, o] for i in range(ai))
                for i in range(ai):
                    cc, k = i // ib, i % ib
                    limit = lim[(rr * C + cc) * ob + j, :, k * BLK : (k + 1) * BLK]
                    value = mixed[i].reshape(ds // d_blocks, d_blocks, BLK)
                    value = jnp.minimum(jnp.maximum(value, -limit), limit)
                    clip[i, o] = value.reshape(ds, BLK).astype(jnp.bfloat16)

            total = None
            for i in range(ai):
                cc, k = i // ib, i % ib
                cols = pl.ds(pl.multiple_of(k * INNER + t * BLK, BLK), BLK)
                cal = jnp.concatenate([calv[cal_slot(rr, cc), :, cols] for rr in range(R)], axis=0)
                term = lax.dot_general(
                    cal, clip[i].reshape(ao * ds, BLK), (((1,), (1,)), ((), ())), preferred_element_type=jnp.float32
                )
                total = term if total is None else total + term
            acc[s] += total

    spot = lax.broadcasted_iota(jnp.int32, perm.shape[1:], 0)
    lane = lax.broadcasted_iota(jnp.int32, perm.shape[1:], 1)
    shift = (pr // H).bit_length() - 1
    step = ds.bit_length() - 1
    for q in range(R):
        for s in range(S):
            wanted = (q * ob + (lane >> shift)) * ds + (lane & (ds - 1))
            hit = (spot == wanted) & (((lane & (pr // H - 1)) >> step) == s % (S // H))
            perm[q * S + s] = jnp.where(hit, 1.0, 0.0).astype(jnp.bfloat16)
    acc[...] = jnp.zeros_like(acc)

    @pl.loop(0, chunks + SEND_SLOTS)
    def _(i):
        slot = lax.rem(i, SEND_SLOTS)

        @pl.when(i >= SEND_SLOTS)
        def _():
            wait_own(slot)

        @pl.when(i < chunks)
        def _():
            @pl.when(i >= SEND_SLOTS)
            def _():
                wait_send(slot)

            inner(i, slot)
            send(i, slot)

        for at in range(SEND_SLOTS + 1):
            @pl.when(i == at)
            def _():
                cal_advance(at)
                if at == SEND_SLOTS:
                    for later in range(at + 1, stages):
                        cal_advance(later)
                    read_levels()

        @pl.when(i >= SEND_SLOTS)
        def _():
            outer(i - SEND_SLOTS)

    finish(H - 1)
    send_out(H - 1)

    for t in range(chunks - SEND_SLOTS, chunks):
        wait_send(t % SEND_SLOTS)
    for stage in range(stages):
        cal_copy(stage).wait_send()
    sent = levv.at[pl.ds(0, n - 1)]
    pltpu.make_async_copy(sent, sent, lev_send).wait()
    for h in range(H):
        pltpu.make_async_copy(out_ref.at[h], out_ref.at[h], out_recv.at[h]).wait()
        sent = ostage.at[h, pl.ds(0, n - 1)]
        pltpu.make_async_copy(sent, sent, out_send.at[h]).wait()


def shards(query_weight, sign_input, sign_output, clip_level, calibration):
    rows_local, cols_local = query_weight.shape
    R, C = lax.axis_size("row"), lax.axis_size("col")
    n = R * C
    ob, ib = rows_local // INNER, cols_local // INNER
    pr = INNER // n
    ds = min(16, pr)
    S = pr // ds
    H = 2 if S % 2 == 0 else 1
    chunks = INNER // BLK
    cal_local = calibration.shape[0]
    cal_rows = R * cal_local
    ao, ai = R * ob, C * ib
    wide = ib * BLK
    stages = len(bits_of(R)) + len(bits_of(C))
    bf16, f32 = jnp.bfloat16, jnp.float32

    _, result = pl.pallas_call(
        functools.partial(kernel, R, C),
        in_specs=[
            pl.BlockSpec(memory_space=pl.ANY),
            pl.BlockSpec(memory_space=pl.ANY),
            pl.BlockSpec(memory_space=pl.ANY),
            pl.BlockSpec(memory_space=pl.ANY),
            pl.BlockSpec(memory_space=pl.ANY),
        ],
        out_specs=[pl.BlockSpec(memory_space=pl.ANY)] * 2,
        out_shape=[
            jax.ShapeDtypeStruct((chunks * S, n, ob, ds, wide), bf16),
            jax.ShapeDtypeStruct((H, n, cal_rows // C, ob * pr // H), bf16),
        ],
        scratch_shapes=[
            pltpu.VMEM((ib, 1, INNER), jnp.int32),
            pltpu.VMEM((ob, 1, INNER), jnp.int32),
            pltpu.VMEM((ob, INNER, INNER), bf16),
            pltpu.VMEM((ib, INNER, BLK), bf16),
            pltpu.VMEM((ib, INNER, BLK), bf16),
            pltpu.VMEM((WEIGHT_SLOTS, INNER, INNER), bf16),
            pltpu.VMEM((INNER, wide), bf16),
            pltpu.VMEM((SEND_SLOTS, n, S, ob, ds, wide), bf16),
            pltpu.VMEM((n, ob, ds, wide), bf16),
            pltpu.VMEM((ai, ao, ds, BLK), f32),
            pltpu.VMEM((ai, ao, ds, BLK), bf16),
            pltpu.VMEM((S, cal_rows, ao * ds), f32),
            pltpu.VMEM((S, cal_rows, ao * ds), bf16),
            pltpu.VMEM((R * S, ao * ds, ob * pr // H), bf16),
            pltpu.VMEM((n, cal_local, cols_local), bf16),
            pltpu.VMEM((n,) + clip_level.shape, jnp.int32),
            pltpu.VMEM((n * clip_level.shape[0], clip_level.shape[1]), bf16),
            pltpu.VMEM((n * ob, INNER // BLK, wide), f32),
            pltpu.VMEM((H, n, cal_rows // C, ob * pr // H), bf16),
            pltpu.SemaphoreType.DMA((2,)),
            pltpu.SemaphoreType.DMA((WEIGHT_SLOTS,)),
            pltpu.SemaphoreType.DMA((SEND_SLOTS,)),
            pltpu.SemaphoreType.DMA((SEND_SLOTS,)),
            pltpu.SemaphoreType.DMA((chunks * S,)),
            pltpu.SemaphoreType.DMA,
            pltpu.SemaphoreType.DMA,
            pltpu.SemaphoreType.DMA((max(stages, 1),)),
            pltpu.SemaphoreType.DMA((max(stages, 1),)),
            pltpu.SemaphoreType.DMA,
            pltpu.SemaphoreType.DMA,
            pltpu.SemaphoreType.DMA((H,)),
            pltpu.SemaphoreType.DMA((H,)),
        ],
        compiler_params=pltpu.CompilerParams(
            collective_id=0, has_side_effects=True, vmem_limit_bytes=60 * 2**20
        ),
    )(query_weight, sign_input.reshape(ib, 1, INNER), sign_output.reshape(ob, 1, INNER), clip_level, calibration)

    result = result.reshape(H, n, cal_rows // C, ob, pr // H)
    return result.transpose(2, 3, 1, 0, 4).reshape(cal_rows // C, rows_local)


def solution(mesh):
    placed = (
        P(("layer", "row"), "col"),
        P(("layer", "col")),
        P(("layer", "row")),
        P(("layer", "row"), "col"),
        P(("layer", "row"), "col"),
    )
    return jax.shard_map(
        shards, mesh=mesh, in_specs=placed, out_specs=P(("layer", "col"), "row"), check_vma=False
    )
```

```python
import functools

import jax
import jax.numpy as jnp
from jax import lax
from jax.experimental import pallas as pl
from jax.experimental.pallas import tpu as pltpu
from jax.sharding import PartitionSpec as P

INNER = 1024
D = 16384
BLK = 128
LEVEL_UNIT = 512
GROUP = 256
SEND_SLOTS = 3
WEIGHT_SLOTS = 3
MESH = pl.DeviceIdType.MESH


def bits_of(size):
    bits = []
    while size > 1:
        size //= 2
        bits.append(size)
    return bits


def mixed_order(n, i):
    return n // 2 * lax.rem(i, 2) + i // 2


def flip(at, bit):
    return at + bit * (1 - 2 * lax.rem(at // bit, 2))


def exclusive_or(a, b, size):
    total = 0
    for bit in bits_of(size):
        total = total + bit * lax.rem(a // bit + b // bit, 2)
    return total


def sylvester(size):
    x = lax.broadcasted_iota(jnp.int32, (size, size), 0) & lax.broadcasted_iota(jnp.int32, (size, size), 1)
    x = x ^ (x >> 4)
    x = x ^ (x >> 2)
    x = x ^ (x >> 1)
    return (1 - 2 * (x & 1)).astype(jnp.float32)


def butterfly(values):
    values = list(values)
    half = 1
    while half < len(values):
        for at in range(len(values)):
            if not at & half:
                low, high = values[at], values[at + half]
                values[at], values[at + half] = low + high, low - high
        half *= 2
    return values


def kernel(
    R, C, w_ref, si_hbm, so_hbm, level_ref, cal_ref, recv_ref, out_ref,
    si_ref, so_ref, kout, skin, kin, wbuf, right, sbuf, rbuf, mix, clip, acc, accb, perm, calv, levv, levb, lim, ostage,
    sign_sem, wsem, ssem, own_sem, rsem, usem, cal_own, cal_send, cal_recv, lev_own, lev_send, lev_recv, out_send, out_recv,
):
    layer, r, c = lax.axis_index("layer"), lax.axis_index("row"), lax.axis_index("col")
    n = R * C
    me = r * C + c
    units, _, ob, ds, wide = recv_ref.shape
    ib = wide // BLK
    chunks = INNER // BLK
    S = units // chunks
    H = out_ref.shape[0]
    last = chunks - 1
    pr = S * ds
    ao, ai = R * ob, C * ib
    groups = INNER // BLK
    blocks = ob * ib
    lev_cols = level_ref.shape[1]
    row_bits, col_bits = bits_of(R), bits_of(C)
    stages = len(row_bits) + len(col_bits)

    def peer(i):
        pr_, pc_ = exclusive_or(r, i // C, R), exclusive_or(c, lax.rem(i, C), C)
        return (layer, pr_, pc_), pr_ * C + pc_

    def w_copy(q):
        block, slot = lax.rem(q, blocks), lax.rem(q, WEIGHT_SLOTS)
        rows = pl.ds(pl.multiple_of((block // ib) * INNER, INNER), INNER)
        cols = pl.ds(pl.multiple_of(lax.rem(block, ib) * INNER, INNER), INNER)
        return pltpu.make_async_copy(w_ref.at[rows, cols], wbuf.at[slot], wsem.at[slot])

    def held_slot(rr, cc):
        slot, weight = 0, 1
        for bit in row_bits:
            slot = slot + weight * lax.rem(r // bit + rr // bit, 2)
            weight *= 2
        for bit in col_bits:
            slot = slot + weight * lax.rem(c // bit + cc // bit, 2)
            weight *= 2
        return slot

    def spread(stage, held, own_ref, send_sem, recv_sem):
        size = 2**stage
        if stage < len(row_bits):
            target = (layer, flip(r, row_bits[stage]), c)
        else:
            target = (layer, r, flip(c, col_bits[stage - len(row_bits)]))
        return pltpu.make_async_remote_copy(
            src_ref=own_ref if stage == 0 else held.at[pl.ds(0, size)],
            dst_ref=held.at[1] if stage == 0 else held.at[pl.ds(size, size)],
            send_sem=send_sem.at[stage],
            recv_sem=recv_sem.at[stage],
            device_id=target,
            device_id_type=MESH,
        )

    def stage_copies(stage):
        return (
            spread(stage, levv, level_ref, lev_send, lev_recv),
            spread(stage, calv, cal_ref, cal_send, cal_recv),
        )

    own_copies = (
        pltpu.make_async_copy(level_ref, levv.at[0], lev_own),
        pltpu.make_async_copy(cal_ref, calv.at[0], cal_own),
    )

    def advance(stage):
        if stage >= stages:
            return
        if stage == 0:
            for copy in own_copies:
                copy.wait()
        for copy in stage_copies(stage):
            copy.wait_recv()
        if stage + 1 < stages:
            for copy in stage_copies(stage + 1):
                copy.start()

    barrier = pltpu.get_barrier_semaphore()

    @pl.loop(1, n)
    def _(i):
        target, _ = peer(i)
        pl.semaphore_signal(barrier, inc=1, device_id=target, device_id_type=MESH)

    sign_copies = [
        pltpu.make_async_copy(si_hbm, si_ref, sign_sem.at[0]),
        pltpu.make_async_copy(so_hbm, so_ref, sign_sem.at[1]),
    ]
    for copy in sign_copies:
        copy.start()
    for copy in own_copies:
        copy.start()
    for q in range(WEIGHT_SLOTS - 1):
        w_copy(q).start()
    pl.semaphore_wait(barrier, n - 1)

    if stages:
        for copy in stage_copies(0):
            copy.start()

    table = sylvester(BLK)
    table_b = table.astype(jnp.bfloat16)
    diagonal = lax.broadcasted_iota(jnp.int32, (BLK, BLK), 0) == lax.broadcasted_iota(jnp.int32, (BLK, BLK), 1)

    for copy in sign_copies:
        copy.wait()

    def static_sign(a, b):
        return 1.0 - 2.0 * (bin(a & b).count("1") & 1)

    @pl.loop(0, ib)
    def _(k):
        for g in range(groups):
            signs = si_ref[k, :, g * BLK : (g + 1) * BLK].astype(jnp.float32)
            scaled = jnp.where(diagonal, signs, 0.0).astype(jnp.bfloat16)
            skin[k, g * BLK : (g + 1) * BLK, :] = jnp.dot(
                scaled, table_b, preferred_element_type=jnp.float32
            ).astype(jnp.bfloat16)

    @pl.loop(0, ob)
    def _(j):
        for g in range(groups):
            signs = so_ref[j, :, g * BLK : (g + 1) * BLK].astype(jnp.float32)
            plus = (table * signs).astype(jnp.bfloat16)
            minus = (table * -signs).astype(jnp.bfloat16)
            for h in range(groups):
                kout[j, h * BLK : (h + 1) * BLK, g * BLK : (g + 1) * BLK] = plus if static_sign(g, h) > 0 else minus

    def inner(t, slot):
        for g in range(groups):
            parity = 0
            for bit in bits_of(groups):
                if g & bit:
                    parity = parity + lax.rem(t // bit, 2)
            sign = (1 - 2 * lax.rem(parity + 0 * t, 2)).astype(jnp.float32)
            for k in range(ib):
                rows = slice(g * BLK, (g + 1) * BLK)
                kin[k, rows, :] = (skin[k, rows, :].astype(jnp.float32) * sign).astype(jnp.bfloat16)

        @pl.loop(0, ob)
        def _(j):
            @pl.loop(0, ib)
            def _(k):
                q = (t * ob + j) * ib + k
                w_copy(q).wait()

                @pl.when(q + WEIGHT_SLOTS - 1 < chunks * blocks)
                def _():
                    w_copy(q + WEIGHT_SLOTS - 1).start()

                wslot = lax.rem(q, WEIGHT_SLOTS)

                @pl.loop(0, INNER // GROUP)
                def _(m):
                    rows = pl.ds(pl.multiple_of(m * GROUP, GROUP), GROUP)
                    cols = pl.ds(pl.multiple_of(k * BLK, BLK), BLK)
                    right[rows, cols] = jnp.dot(
                        wbuf[wslot, rows, :], kin[k], preferred_element_type=jnp.float32
                    ).astype(jnp.bfloat16)

            @pl.loop(0, INNER // GROUP)
            def _(m):
                rows = pl.ds(pl.multiple_of(m * GROUP, GROUP), GROUP)
                both = jnp.dot(kout[j, rows, :], right[...], preferred_element_type=jnp.float32)
                per = GROUP // pr
                sbuf[slot, pl.ds(m * per, per), :, j] = both.reshape(per, S, ds, wide).astype(jnp.bfloat16)

    def send(t, slot):
        @pl.loop(0, S)
        def _(s):
            u = t * S + s
            pltpu.make_async_copy(sbuf.at[slot, me, s], recv_ref.at[u, me], own_sem.at[slot]).start()

            @pl.loop(1, n)
            def _(i):
                target, place = peer(mixed_order(n, i))
                pltpu.make_async_remote_copy(
                    src_ref=sbuf.at[slot, place, s], dst_ref=recv_ref.at[u, me],
                    send_sem=ssem.at[slot], recv_sem=rsem.at[u],
                    device_id=target, device_id_type=MESH,
                ).start()

    def wait_send(slot):
        sent = sbuf.at[slot, pl.ds(0, n - 1)]
        pltpu.make_async_copy(sent, sent, ssem.at[slot]).wait()

    def wait_own(slot):
        own = sbuf.at[slot, me]
        pltpu.make_async_copy(own, own, own_sem.at[slot]).wait()

    d_block = me * pr // BLK
    d_blocks = INNER // BLK

    def read_levels():
        level = levv[...].astype(jnp.float32).reshape(n * ob, d_blocks, lev_cols)
        line = lax.broadcasted_iota(jnp.int32, level.shape, 1)
        level = jnp.sum(jnp.where(line == d_block, level, 0.0), axis=1, keepdims=True)
        level = jnp.broadcast_to(level, (n * ob, d_blocks, lev_cols)).reshape(n * ob * d_blocks, lev_cols)
        levb[...] = level.astype(jnp.bfloat16)

    def finish(h):
        own_units = range(h * (S // H), (h + 1) * (S // H))
        rows_each = ostage.shape[2]
        for s in own_units:
            accb[s] = (acc[s] * (1.0 / D)).astype(jnp.bfloat16)

        @pl.loop(0, R)
        def _(q):
            total = None
            for s in own_units:
                term = jnp.dot(accb[s], perm[q * S + s], preferred_element_type=jnp.float32)
                total = term if total is None else total + term
            for cc in range(C):
                ostage[h, q * C + cc] = total[cc * rows_each : (cc + 1) * rows_each].astype(jnp.bfloat16)

    def send_out(h):
        pltpu.make_async_copy(ostage.at[h, me], out_ref.at[h, me], out_recv.at[h]).start()

        @pl.loop(1, n)
        def _(i):
            target, place = peer(n - i)
            pltpu.make_async_remote_copy(
                src_ref=ostage.at[h, place], dst_ref=out_ref.at[h, me],
                send_sem=out_send.at[h], recv_sem=out_recv.at[h],
                device_id=target, device_id_type=MESH,
            ).start()

    def outer(t):
        lane = lax.broadcasted_iota(jnp.int32, (lev_cols, wide), 1)
        line = lax.broadcasted_iota(jnp.int32, (lev_cols, wide), 0)
        pick = jnp.where(line == (lane >> 7) * d_blocks + t, float(D // LEVEL_UNIT), 0.0).astype(jnp.bfloat16)
        lim[...] = jnp.dot(levb[...], pick, preferred_element_type=jnp.float32).reshape(lim.shape)

        @pl.loop(0, S)
        def _(s):
            u = t * S + s
            final_unit = (t == last) & (s == S - 1)
            if H > 1:
                @pl.when(final_unit)
                def _():
                    finish(0)

            arrived = recv_ref.at[u, pl.ds(0, n - 1)]
            pltpu.make_async_copy(arrived, arrived, rsem.at[u]).wait()
            if H > 1:
                @pl.when(final_unit)
                def _():
                    send_out(0)

            fetch = pltpu.make_async_copy(recv_ref.at[u], rbuf, usem)
            fetch.start()
            fetch.wait()

            @pl.loop(0, ai)
            def _(i):
                cc, k = i // ib, lax.rem(i, ib)
                cols = pl.ds(pl.multiple_of(k * BLK, BLK), BLK)
                mixed = butterfly(
                    rbuf[rr * C + cc, j, :, cols].astype(jnp.float32) for rr in range(R) for j in range(ob)
                )
                for o in range(ao):
                    mix[i, o] = mixed[o]

            @pl.loop(0, ao)
            def _(o):
                rr, j = o // ob, lax.rem(o, ob)
                slots = [held_slot(rr, cc) for cc in range(C)]
                mixed = butterfly(mix[i, o] for i in range(ai))
                for i in range(ai):
                    cc, k = i // ib, i % ib
                    limit = lim[slots[cc] * ob + j, :, k * BLK : (k + 1) * BLK]
                    value = mixed[i].reshape(ds // d_blocks, d_blocks, BLK)
                    value = jnp.minimum(jnp.maximum(value, -limit), limit)
                    clip[i, o] = value.reshape(ds, BLK).astype(jnp.bfloat16)

            total = None
            for i in range(ai):
                cc, k = i // ib, i % ib
                cols = pl.ds(pl.multiple_of(k * INNER + t * BLK, BLK), BLK)
                cal = jnp.concatenate([calv[held_slot(rr, cc), :, cols] for rr in range(R)], axis=0)
                term = lax.dot_general(
                    cal, clip[i].reshape(ao * ds, BLK), (((1,), (1,)), ((), ())), preferred_element_type=jnp.float32
                )
                total = term if total is None else total + term
            acc[s] += total

    spot = lax.broadcasted_iota(jnp.int32, perm.shape[1:], 0)
    lane = lax.broadcasted_iota(jnp.int32, perm.shape[1:], 1)
    shift = (pr // H).bit_length() - 1
    step = ds.bit_length() - 1
    for q in range(R):
        for s in range(S):
            wanted = (q * ob + (lane >> shift)) * ds + (lane & (ds - 1))
            hit = (spot == wanted) & (((lane & (pr // H - 1)) >> step) == s % (S // H))
            perm[q * S + s] = jnp.where(hit, 1.0, 0.0).astype(jnp.bfloat16)
    acc[...] = jnp.zeros_like(acc)

    @pl.loop(0, chunks + SEND_SLOTS)
    def _(i):
        slot = lax.rem(i, SEND_SLOTS)

        @pl.when(i >= SEND_SLOTS)
        def _():
            wait_own(slot)

        @pl.when(i < chunks)
        def _():
            @pl.when(i >= SEND_SLOTS)
            def _():
                wait_send(slot)

            inner(i, slot)
            send(i, slot)

        for at in range(SEND_SLOTS + 1):
            @pl.when(i == at)
            def _():
                advance(at)
                if at == SEND_SLOTS:
                    for later in range(at + 1, stages):
                        advance(later)
                    read_levels()

        @pl.when(i >= SEND_SLOTS)
        def _():
            outer(i - SEND_SLOTS)

    finish(H - 1)
    send_out(H - 1)

    for t in range(chunks - SEND_SLOTS, chunks):
        wait_send(t % SEND_SLOTS)
    for stage in range(stages):
        for copy in stage_copies(stage):
            copy.wait_send()
    for h in range(H):
        pltpu.make_async_copy(out_ref.at[h], out_ref.at[h], out_recv.at[h]).wait()
        sent = ostage.at[h, pl.ds(0, n - 1)]
        pltpu.make_async_copy(sent, sent, out_send.at[h]).wait()


def shards(query_weight, sign_input, sign_output, clip_level, calibration):
    rows_local, cols_local = query_weight.shape
    R, C = lax.axis_size("row"), lax.axis_size("col")
    n = R * C
    ob, ib = rows_local // INNER, cols_local // INNER
    pr = INNER // n
    ds = min(16, pr)
    S = pr // ds
    H = 2 if S % 2 == 0 else 1
    chunks = INNER // BLK
    cal_local = calibration.shape[0]
    cal_rows = R * cal_local
    ao, ai = R * ob, C * ib
    wide = ib * BLK
    stages = len(bits_of(R)) + len(bits_of(C))
    bf16, f32 = jnp.bfloat16, jnp.float32

    _, result = pl.pallas_call(
        functools.partial(kernel, R, C),
        in_specs=[
            pl.BlockSpec(memory_space=pl.ANY),
            pl.BlockSpec(memory_space=pl.ANY),
            pl.BlockSpec(memory_space=pl.ANY),
            pl.BlockSpec(memory_space=pl.ANY),
            pl.BlockSpec(memory_space=pl.ANY),
        ],
        out_specs=[pl.BlockSpec(memory_space=pl.ANY)] * 2,
        out_shape=[
            jax.ShapeDtypeStruct((chunks * S, n, ob, ds, wide), bf16),
            jax.ShapeDtypeStruct((H, n, cal_rows // C, ob * pr // H), bf16),
        ],
        scratch_shapes=[
            pltpu.VMEM((ib, 1, INNER), jnp.int32),
            pltpu.VMEM((ob, 1, INNER), jnp.int32),
            pltpu.VMEM((ob, INNER, INNER), bf16),
            pltpu.VMEM((ib, INNER, BLK), bf16),
            pltpu.VMEM((ib, INNER, BLK), bf16),
            pltpu.VMEM((WEIGHT_SLOTS, INNER, INNER), bf16),
            pltpu.VMEM((INNER, wide), bf16),
            pltpu.VMEM((SEND_SLOTS, n, S, ob, ds, wide), bf16),
            pltpu.VMEM((n, ob, ds, wide), bf16),
            pltpu.VMEM((ai, ao, ds, BLK), f32),
            pltpu.VMEM((ai, ao, ds, BLK), bf16),
            pltpu.VMEM((S, cal_rows, ao * ds), f32),
            pltpu.VMEM((S, cal_rows, ao * ds), bf16),
            pltpu.VMEM((R * S, ao * ds, ob * pr // H), bf16),
            pltpu.VMEM((n, cal_local, cols_local), bf16),
            pltpu.VMEM((n,) + clip_level.shape, jnp.int32),
            pltpu.VMEM((n * clip_level.shape[0], clip_level.shape[1]), bf16),
            pltpu.VMEM((n * ob, INNER // BLK, wide), f32),
            pltpu.VMEM((H, n, cal_rows // C, ob * pr // H), bf16),
            pltpu.SemaphoreType.DMA((2,)),
            pltpu.SemaphoreType.DMA((WEIGHT_SLOTS,)),
            pltpu.SemaphoreType.DMA((SEND_SLOTS,)),
            pltpu.SemaphoreType.DMA((SEND_SLOTS,)),
            pltpu.SemaphoreType.DMA((chunks * S,)),
            pltpu.SemaphoreType.DMA,
            pltpu.SemaphoreType.DMA,
            pltpu.SemaphoreType.DMA((max(stages, 1),)),
            pltpu.SemaphoreType.DMA((max(stages, 1),)),
            pltpu.SemaphoreType.DMA,
            pltpu.SemaphoreType.DMA((max(stages, 1),)),
            pltpu.SemaphoreType.DMA((max(stages, 1),)),
            pltpu.SemaphoreType.DMA((H,)),
            pltpu.SemaphoreType.DMA((H,)),
        ],
        compiler_params=pltpu.CompilerParams(
            collective_id=0, has_side_effects=True, vmem_limit_bytes=60 * 2**20
        ),
    )(query_weight, sign_input.reshape(ib, 1, INNER), sign_output.reshape(ob, 1, INNER), clip_level, calibration)

    result = result.reshape(H, n, cal_rows // C, ob, pr // H)
    return result.transpose(2, 3, 1, 0, 4).reshape(cal_rows // C, rows_local)


def solution(mesh):
    placed = (
        P(("layer", "row"), "col"),
        P(("layer", "col")),
        P(("layer", "row")),
        P(("layer", "row"), "col"),
        P(("layer", "row"), "col"),
    )
    return jax.shard_map(
        shards, mesh=mesh, in_specs=placed, out_specs=P(("layer", "col"), "row"), check_vma=False
    )
```

```python
import functools

import jax
import jax.numpy as jnp
from jax import lax
from jax.experimental import pallas as pl
from jax.experimental.pallas import tpu as pltpu
from jax.sharding import PartitionSpec as P

INNER = 1024
D = 16384
BLK = 128
LEVEL_UNIT = 512
GROUP = 256
SEND_SLOTS = 3
WEIGHT_SLOTS = 3
MESH = pl.DeviceIdType.MESH


def bits_of(size):
    bits = []
    while size > 1:
        size //= 2
        bits.append(size)
    return bits


def mixed_order(n, i):
    return n // 2 * lax.rem(i, 2) + i // 2


def flip(at, bit):
    return at + bit * (1 - 2 * lax.rem(at // bit, 2))


def exclusive_or(a, b, size):
    total = 0
    for bit in bits_of(size):
        total = total + bit * lax.rem(a // bit + b // bit, 2)
    return total


def sylvester(size):
    x = lax.broadcasted_iota(jnp.int32, (size, size), 0) & lax.broadcasted_iota(jnp.int32, (size, size), 1)
    x = x ^ (x >> 4)
    x = x ^ (x >> 2)
    x = x ^ (x >> 1)
    return (1 - 2 * (x & 1)).astype(jnp.float32)


def butterfly(values):
    values = list(values)
    half = 1
    while half < len(values):
        for at in range(len(values)):
            if not at & half:
                low, high = values[at], values[at + half]
                values[at], values[at + half] = low + high, low - high
        half *= 2
    return values


def kernel(
    R, C, w_ref, si_hbm, so_hbm, level_ref, cal_ref, recv_ref, out_ref,
    si_ref, so_ref, kout, skin, kin, wbuf, right, sbuf, rbuf, mix, clip, acc, accb, perm, calv, levv, levb, lim, ostage,
    sign_sem, wsem, ssem, own_sem, rsem, usem, cal_own, cal_send, cal_recv, lev_own, lev_send, lev_recv, out_send, out_recv,
):
    layer, r, c = lax.axis_index("layer"), lax.axis_index("row"), lax.axis_index("col")
    n = R * C
    me = r * C + c
    units, _, ob, ds, wide = recv_ref.shape
    ib = wide // BLK
    chunks = INNER // BLK
    S = units // chunks
    H = out_ref.shape[0]
    last = chunks - 1
    pr = S * ds
    ao, ai = R * ob, C * ib
    groups = INNER // BLK
    blocks = ob * ib
    lev_cols = level_ref.shape[1]
    row_bits, col_bits = bits_of(R), bits_of(C)
    stages = len(row_bits) + len(col_bits)

    def peer(i):
        pr_, pc_ = exclusive_or(r, i // C, R), exclusive_or(c, lax.rem(i, C), C)
        return (layer, pr_, pc_), pr_ * C + pc_

    def w_copy(q):
        block, slot = lax.rem(q, blocks), lax.rem(q, WEIGHT_SLOTS)
        rows = pl.ds(pl.multiple_of((block // ib) * INNER, INNER), INNER)
        cols = pl.ds(pl.multiple_of(lax.rem(block, ib) * INNER, INNER), INNER)
        return pltpu.make_async_copy(w_ref.at[rows, cols], wbuf.at[slot], wsem.at[slot])

    def held_slot(rr, cc):
        slot, weight = 0, 1
        for bit in row_bits:
            slot = slot + weight * lax.rem(r // bit + rr // bit, 2)
            weight *= 2
        for bit in col_bits:
            slot = slot + weight * lax.rem(c // bit + cc // bit, 2)
            weight *= 2
        return slot

    def spread(stage, held, own_ref, send_sem, recv_sem):
        size = 2**stage
        if stage < len(row_bits):
            target = (layer, flip(r, row_bits[stage]), c)
        else:
            target = (layer, r, flip(c, col_bits[stage - len(row_bits)]))
        return pltpu.make_async_remote_copy(
            src_ref=own_ref if stage == 0 else held.at[pl.ds(0, size)],
            dst_ref=held.at[1] if stage == 0 else held.at[pl.ds(size, size)],
            send_sem=send_sem.at[stage],
            recv_sem=recv_sem.at[stage],
            device_id=target,
            device_id_type=MESH,
        )

    def stage_copies(stage):
        return (
            spread(stage, levv, level_ref, lev_send, lev_recv),
            spread(stage, calv, cal_ref, cal_send, cal_recv),
        )

    own_copies = (
        pltpu.make_async_copy(level_ref, levv.at[0], lev_own),
        pltpu.make_async_copy(cal_ref, calv.at[0], cal_own),
    )

    def advance(stage):
        if stage >= stages:
            return
        if stage == 0:
            for copy in own_copies:
                copy.wait()
        for copy in stage_copies(stage):
            copy.wait_recv()
        if stage + 1 < stages:
            for copy in stage_copies(stage + 1):
                copy.start()

    barrier = pltpu.get_barrier_semaphore()

    @pl.loop(1, n)
    def _(i):
        target, _ = peer(i)
        pl.semaphore_signal(barrier, inc=1, device_id=target, device_id_type=MESH)

    sign_copies = [
        pltpu.make_async_copy(si_hbm, si_ref, sign_sem.at[0]),
        pltpu.make_async_copy(so_hbm, so_ref, sign_sem.at[1]),
    ]
    for copy in sign_copies:
        copy.start()
    for copy in own_copies:
        copy.start()
    for q in range(WEIGHT_SLOTS - 1):
        w_copy(q).start()
    pl.semaphore_wait(barrier, n - 1)

    if stages:
        for copy in stage_copies(0):
            copy.start()

    table = sylvester(BLK)
    table_b = table.astype(jnp.bfloat16)
    diagonal = lax.broadcasted_iota(jnp.int32, (BLK, BLK), 0) == lax.broadcasted_iota(jnp.int32, (BLK, BLK), 1)

    for copy in sign_copies:
        copy.wait()

    def static_sign(a, b):
        return 1.0 - 2.0 * (bin(a & b).count("1") & 1)

    @pl.loop(0, ib)
    def _(k):
        for g in range(groups):
            signs = si_ref[k, :, g * BLK : (g + 1) * BLK].astype(jnp.float32)
            scaled = jnp.where(diagonal, signs, 0.0).astype(jnp.bfloat16)
            skin[k, g * BLK : (g + 1) * BLK, :] = jnp.dot(
                scaled, table_b, preferred_element_type=jnp.float32
            ).astype(jnp.bfloat16)

    @pl.loop(0, ob)
    def _(j):
        for g in range(groups):
            signs = so_ref[j, :, g * BLK : (g + 1) * BLK].astype(jnp.float32)
            plus = (table * signs).astype(jnp.bfloat16)
            minus = (table * -signs).astype(jnp.bfloat16)
            for h in range(groups):
                kout[j, h * BLK : (h + 1) * BLK, g * BLK : (g + 1) * BLK] = plus if static_sign(g, h) > 0 else minus

    def inner(t, slot):
        for g in range(groups):
            parity = 0
            for bit in bits_of(groups):
                if g & bit:
                    parity = parity + lax.rem(t // bit, 2)
            sign = (1 - 2 * lax.rem(parity + 0 * t, 2)).astype(jnp.float32)
            for k in range(ib):
                rows = slice(g * BLK, (g + 1) * BLK)
                kin[k, rows, :] = (skin[k, rows, :].astype(jnp.float32) * sign).astype(jnp.bfloat16)

        @pl.loop(0, ob)
        def _(j):
            @pl.loop(0, ib)
            def _(k):
                q = (t * ob + j) * ib + k
                w_copy(q).wait()

                @pl.when(q + WEIGHT_SLOTS - 1 < chunks * blocks)
                def _():
                    w_copy(q + WEIGHT_SLOTS - 1).start()

                wslot = lax.rem(q, WEIGHT_SLOTS)

                @pl.loop(0, INNER // GROUP)
                def _(m):
                    rows = pl.ds(pl.multiple_of(m * GROUP, GROUP), GROUP)
                    cols = pl.ds(pl.multiple_of(k * BLK, BLK), BLK)
                    right[rows, cols] = jnp.dot(
                        wbuf[wslot, rows, :], kin[k], preferred_element_type=jnp.float32
                    ).astype(jnp.bfloat16)

            @pl.loop(0, INNER // GROUP)
            def _(m):
                rows = pl.ds(pl.multiple_of(m * GROUP, GROUP), GROUP)
                both = jnp.dot(kout[j, rows, :], right[...], preferred_element_type=jnp.float32)
                per = GROUP // pr
                sbuf[slot, pl.ds(m * per, per), :, j] = both.reshape(per, S, ds, wide).astype(jnp.bfloat16)

    def send(t, slot):
        @pl.loop(0, S)
        def _(s):
            u = t * S + s
            pltpu.make_async_copy(sbuf.at[slot, me, s], recv_ref.at[u, me], own_sem.at[slot]).start()

            @pl.loop(1, n)
            def _(i):
                target, place = peer(mixed_order(n, i))
                pltpu.make_async_remote_copy(
                    src_ref=sbuf.at[slot, place, s], dst_ref=recv_ref.at[u, me],
                    send_sem=ssem.at[slot], recv_sem=rsem.at[u],
                    device_id=target, device_id_type=MESH,
                ).start()

    def wait_send(slot):
        sent = sbuf.at[slot, pl.ds(0, n - 1)]
        pltpu.make_async_copy(sent, sent, ssem.at[slot]).wait()

    def wait_own(slot):
        own = sbuf.at[slot, me]
        pltpu.make_async_copy(own, own, own_sem.at[slot]).wait()

    d_block = me * pr // BLK
    d_blocks = INNER // BLK

    def read_levels():
        level = levv[...].astype(jnp.float32).reshape(n * ob, d_blocks, lev_cols)
        line = lax.broadcasted_iota(jnp.int32, level.shape, 1)
        level = jnp.sum(jnp.where(line == d_block, level, 0.0), axis=1, keepdims=True)
        level = jnp.broadcast_to(level, (n * ob, d_blocks, lev_cols)).reshape(n * ob * d_blocks, lev_cols)
        levb[...] = level.astype(jnp.bfloat16)

    def finish(h):
        own_units = range(h * (S // H), (h + 1) * (S // H))
        rows_each = ostage.shape[2]
        for s in own_units:
            accb[s] = (acc[s] * (1.0 / D)).astype(jnp.bfloat16)

        @pl.loop(0, R)
        def _(q):
            total = None
            for s in own_units:
                term = jnp.dot(accb[s], perm[q * S + s], preferred_element_type=jnp.float32)
                total = term if total is None else total + term
            for cc in range(C):
                ostage[h, q * C + cc] = total[cc * rows_each : (cc + 1) * rows_each].astype(jnp.bfloat16)

    def send_out(h):
        pltpu.make_async_copy(ostage.at[h, me], out_ref.at[h, me], out_recv.at[h]).start()

        @pl.loop(1, n)
        def _(i):
            target, place = peer(n - i)
            pltpu.make_async_remote_copy(
                src_ref=ostage.at[h, place], dst_ref=out_ref.at[h, me],
                send_sem=out_send.at[h], recv_sem=out_recv.at[h],
                device_id=target, device_id_type=MESH,
            ).start()

    def outer(t):
        lane = lax.broadcasted_iota(jnp.int32, (lev_cols, wide), 1)
        line = lax.broadcasted_iota(jnp.int32, (lev_cols, wide), 0)
        pick = jnp.where(line == (lane >> 7) * d_blocks + t, float(D // LEVEL_UNIT), 0.0).astype(jnp.bfloat16)
        lim[...] = jnp.dot(levb[...], pick, preferred_element_type=jnp.float32).reshape(lim.shape)

        @pl.loop(0, S)
        def _(s):
            u = t * S + s
            final_unit = (t == last) & (s == S - 1)
            if H > 1:
                @pl.when(final_unit)
                def _():
                    finish(0)

            arrived = recv_ref.at[u, pl.ds(0, n - 1)]
            pltpu.make_async_copy(arrived, arrived, rsem.at[u]).wait()
            if H > 1:
                @pl.when(final_unit)
                def _():
                    send_out(0)

            fetch = pltpu.make_async_copy(recv_ref.at[u], rbuf, usem)
            fetch.start()
            fetch.wait()

            @pl.loop(0, ai)
            def _(i):
                cc, k = i // ib, lax.rem(i, ib)
                cols = pl.ds(pl.multiple_of(k * BLK, BLK), BLK)
                mixed = butterfly(
                    rbuf[rr * C + cc, j, :, cols].astype(jnp.float32) for rr in range(R) for j in range(ob)
                )
                for o in range(ao):
                    mix[i, o] = mixed[o]

            @pl.loop(0, ao)
            def _(o):
                rr, j = o // ob, lax.rem(o, ob)
                slots = [held_slot(rr, cc) for cc in range(C)]
                mixed = butterfly(mix[i, o] for i in range(ai))
                for i in range(ai):
                    cc, k = i // ib, i % ib
                    limit = lim[slots[cc] * ob + j, :, k * BLK : (k + 1) * BLK]
                    value = mixed[i].reshape(ds // d_blocks, d_blocks, BLK)
                    value = jnp.minimum(jnp.maximum(value, -limit), limit)
                    clip[i, o] = value.reshape(ds, BLK).astype(jnp.bfloat16)

            total = None
            for i in range(ai):
                cc, k = i // ib, i % ib
                cols = pl.ds(pl.multiple_of(k * INNER + t * BLK, BLK), BLK)
                cal = jnp.concatenate([calv[held_slot(rr, cc), :, cols] for rr in range(R)], axis=0)
                term = lax.dot_general(
                    cal, clip[i].reshape(ao * ds, BLK), (((1,), (1,)), ((), ())), preferred_element_type=jnp.float32
                )
                total = term if total is None else total + term
            acc[s] += total

    spot = lax.broadcasted_iota(jnp.int32, perm.shape[1:], 0)
    lane = lax.broadcasted_iota(jnp.int32, perm.shape[1:], 1)
    shift = (pr // H).bit_length() - 1
    step = ds.bit_length() - 1
    for q in range(R):
        for s in range(S):
            turn = lax.rem(me, ob // H) * H + s // (S // H) if perm.shape[2] == BLK else 0
            wanted = (q * ob + (((lane >> shift) + ob - turn) & (ob - 1))) * ds + (lane & (ds - 1))
            hit = (spot == wanted) & (((lane & (pr // H - 1)) >> step) == s % (S // H))
            perm[q * S + s] = jnp.where(hit, 1.0, 0.0).astype(jnp.bfloat16)
    acc[...] = jnp.zeros_like(acc)

    @pl.loop(0, chunks + SEND_SLOTS)
    def _(i):
        slot = lax.rem(i, SEND_SLOTS)

        @pl.when(i >= SEND_SLOTS)
        def _():
            wait_own(slot)

        @pl.when(i < chunks)
        def _():
            @pl.when(i >= SEND_SLOTS)
            def _():
                wait_send(slot)

            inner(i, slot)
            send(i, slot)

        for at in range(SEND_SLOTS + 1):
            @pl.when(i == at)
            def _():
                advance(at)
                if at == SEND_SLOTS:
                    for later in range(at + 1, stages):
                        advance(later)
                    read_levels()

        @pl.when(i >= SEND_SLOTS)
        def _():
            outer(i - SEND_SLOTS)

    finish(H - 1)
    send_out(H - 1)

    for t in range(chunks - SEND_SLOTS, chunks):
        wait_send(t % SEND_SLOTS)
    for stage in range(stages):
        for copy in stage_copies(stage):
            copy.wait_send()
    for h in range(H):
        pltpu.make_async_copy(out_ref.at[h], out_ref.at[h], out_recv.at[h]).wait()
        sent = ostage.at[h, pl.ds(0, n - 1)]
        pltpu.make_async_copy(sent, sent, out_send.at[h]).wait()


def merge_kernel(ob, x_ref, o_ref):
    H, n, rows, _ = x_ref.shape
    width = BLK // ob
    joined = ob // H
    tiles = n // joined
    slot = lax.broadcasted_iota(jnp.int32, (rows, BLK), 1) // width
    for at in range(tiles):
        values = [x_ref[k % H, at * joined + k // H].astype(jnp.float32) for k in range(ob)]
        for j in range(ob):
            merged = values[0]
            for k in range(1, ob):
                merged = jnp.where(slot == (j + k) % ob, values[k], merged)
            if j:
                merged = pltpu.roll(merged, BLK - j * width, 1)
            cols = slice((j * tiles + at) * BLK, (j * tiles + at + 1) * BLK)
            o_ref[:, cols] = merged.astype(jnp.bfloat16)


def shards(query_weight, sign_input, sign_output, clip_level, calibration):
    rows_local, cols_local = query_weight.shape
    R, C = lax.axis_size("row"), lax.axis_size("col")
    n = R * C
    ob, ib = rows_local // INNER, cols_local // INNER
    pr = INNER // n
    ds = min(16, pr)
    S = pr // ds
    H = 2 if S % 2 == 0 else 1
    chunks = INNER // BLK
    cal_local = calibration.shape[0]
    cal_rows = R * cal_local
    ao, ai = R * ob, C * ib
    wide = ib * BLK
    stages = len(bits_of(R)) + len(bits_of(C))
    bf16, f32 = jnp.bfloat16, jnp.float32

    _, result = pl.pallas_call(
        functools.partial(kernel, R, C),
        in_specs=[
            pl.BlockSpec(memory_space=pl.ANY),
            pl.BlockSpec(memory_space=pl.ANY),
            pl.BlockSpec(memory_space=pl.ANY),
            pl.BlockSpec(memory_space=pl.ANY),
            pl.BlockSpec(memory_space=pl.ANY),
        ],
        out_specs=[pl.BlockSpec(memory_space=pl.ANY)] * 2,
        out_shape=[
            jax.ShapeDtypeStruct((chunks * S, n, ob, ds, wide), bf16),
            jax.ShapeDtypeStruct((H, n, cal_rows // C, ob * pr // H), bf16),
        ],
        scratch_shapes=[
            pltpu.VMEM((ib, 1, INNER), jnp.int32),
            pltpu.VMEM((ob, 1, INNER), jnp.int32),
            pltpu.VMEM((ob, INNER, INNER), bf16),
            pltpu.VMEM((ib, INNER, BLK), bf16),
            pltpu.VMEM((ib, INNER, BLK), bf16),
            pltpu.VMEM((WEIGHT_SLOTS, INNER, INNER), bf16),
            pltpu.VMEM((INNER, wide), bf16),
            pltpu.VMEM((SEND_SLOTS, n, S, ob, ds, wide), bf16),
            pltpu.VMEM((n, ob, ds, wide), bf16),
            pltpu.VMEM((ai, ao, ds, BLK), f32),
            pltpu.VMEM((ai, ao, ds, BLK), bf16),
            pltpu.VMEM((S, cal_rows, ao * ds), f32),
            pltpu.VMEM((S, cal_rows, ao * ds), bf16),
            pltpu.VMEM((R * S, ao * ds, ob * pr // H), bf16),
            pltpu.VMEM((n, cal_local, cols_local), bf16),
            pltpu.VMEM((n,) + clip_level.shape, jnp.int32),
            pltpu.VMEM((n * clip_level.shape[0], clip_level.shape[1]), bf16),
            pltpu.VMEM((n * ob, INNER // BLK, wide), f32),
            pltpu.VMEM((H, n, cal_rows // C, ob * pr // H), bf16),
            pltpu.SemaphoreType.DMA((2,)),
            pltpu.SemaphoreType.DMA((WEIGHT_SLOTS,)),
            pltpu.SemaphoreType.DMA((SEND_SLOTS,)),
            pltpu.SemaphoreType.DMA((SEND_SLOTS,)),
            pltpu.SemaphoreType.DMA((chunks * S,)),
            pltpu.SemaphoreType.DMA,
            pltpu.SemaphoreType.DMA,
            pltpu.SemaphoreType.DMA((max(stages, 1),)),
            pltpu.SemaphoreType.DMA((max(stages, 1),)),
            pltpu.SemaphoreType.DMA,
            pltpu.SemaphoreType.DMA((max(stages, 1),)),
            pltpu.SemaphoreType.DMA((max(stages, 1),)),
            pltpu.SemaphoreType.DMA((H,)),
            pltpu.SemaphoreType.DMA((H,)),
        ],
        compiler_params=pltpu.CompilerParams(
            collective_id=0, has_side_effects=True, vmem_limit_bytes=60 * 2**20
        ),
    )(query_weight, sign_input.reshape(ib, 1, INNER), sign_output.reshape(ob, 1, INNER), clip_level, calibration)

    rows_out = cal_rows // C
    if ob * pr // H == BLK:
        block = rows_out // 2 if rows_out % 32 == 0 else rows_out
        return pl.pallas_call(
            functools.partial(merge_kernel, ob),
            grid=(rows_out // block,),
            in_specs=[pl.BlockSpec((H, n, block, BLK), lambda i: (0, 0, i, 0))],
            out_specs=pl.BlockSpec((block, rows_local), lambda i: (i, 0)),
            out_shape=jax.ShapeDtypeStruct((rows_out, rows_local), bf16),
        )(result)
    result = result.reshape(H, n, rows_out, ob, pr // H)
    return result.transpose(2, 3, 1, 0, 4).reshape(rows_out, rows_local)


def solution(mesh):
    placed = (
        P(("layer", "row"), "col"),
        P(("layer", "col")),
        P(("layer", "row")),
        P(("layer", "row"), "col"),
        P(("layer", "row"), "col"),
    )
    return jax.shard_map(
        shards, mesh=mesh, in_specs=placed, out_specs=P(("layer", "col"), "row"), check_vma=False
    )
```

```python
import functools

import jax
import jax.numpy as jnp
from jax import lax
from jax.experimental import pallas as pl
from jax.experimental.pallas import tpu as pltpu
from jax.sharding import PartitionSpec as P

INNER = 1024
D = 16384
BLK = 128
LEVEL_UNIT = 512
GROUP = 256
SEND_SLOTS = 3
WEIGHT_SLOTS = 3
MESH = pl.DeviceIdType.MESH


def bits_of(size):
    bits = []
    while size > 1:
        size //= 2
        bits.append(size)
    return bits


def mixed_order(n, i):
    return n // 2 * lax.rem(i, 2) + i // 2


def flip(at, bit):
    return at + bit * (1 - 2 * lax.rem(at // bit, 2))


def exclusive_or(a, b, size):
    total = 0
    for bit in bits_of(size):
        total = total + bit * lax.rem(a // bit + b // bit, 2)
    return total


def sylvester(size):
    x = lax.broadcasted_iota(jnp.int32, (size, size), 0) & lax.broadcasted_iota(jnp.int32, (size, size), 1)
    x = x ^ (x >> 4)
    x = x ^ (x >> 2)
    x = x ^ (x >> 1)
    return (1 - 2 * (x & 1)).astype(jnp.float32)


def butterfly(values):
    values = list(values)
    half = 1
    while half < len(values):
        for at in range(len(values)):
            if not at & half:
                low, high = values[at], values[at + half]
                values[at], values[at + half] = low + high, low - high
        half *= 2
    return values


def kernel(
    R, C, w_ref, si_hbm, so_hbm, level_ref, cal_ref, recv_ref, out_ref,
    si_ref, so_ref, kout, skin, kin, wbuf, right, sbuf, rbuf, mix, clip, acc, accb, perm, calv, levv, levb, lim, ostage,
    sign_sem, wsem, ssem, own_sem, rsem, usem, cal_own, cal_send, cal_recv, lev_own, lev_send, lev_recv, out_send, out_recv,
):
    layer, r, c = lax.axis_index("layer"), lax.axis_index("row"), lax.axis_index("col")
    n = R * C
    me = r * C + c
    units, _, ob, ds, wide = recv_ref.shape
    ib = wide // BLK
    chunks = INNER // BLK
    S = units // chunks
    H = out_ref.shape[0]
    last = chunks - 1
    pr = S * ds
    ao, ai = R * ob, C * ib
    groups = INNER // BLK
    blocks = ob * ib
    lev_cols = level_ref.shape[1]
    row_bits, col_bits = bits_of(R), bits_of(C)
    stages = len(row_bits) + len(col_bits)

    def peer(i):
        pr_, pc_ = exclusive_or(r, i // C, R), exclusive_or(c, lax.rem(i, C), C)
        return (layer, pr_, pc_), pr_ * C + pc_

    def w_copy(q):
        block, slot = lax.rem(q, blocks), lax.rem(q, WEIGHT_SLOTS)
        rows = pl.ds(pl.multiple_of((block // ib) * INNER, INNER), INNER)
        cols = pl.ds(pl.multiple_of(lax.rem(block, ib) * INNER, INNER), INNER)
        return pltpu.make_async_copy(w_ref.at[rows, cols], wbuf.at[slot], wsem.at[slot])

    def held_slot(rr, cc):
        slot, weight = 0, 1
        for bit in row_bits:
            slot = slot + weight * lax.rem(r // bit + rr // bit, 2)
            weight *= 2
        for bit in col_bits:
            slot = slot + weight * lax.rem(c // bit + cc // bit, 2)
            weight *= 2
        return slot

    def spread(stage, held, own_ref, send_sem, recv_sem):
        size = 2**stage
        if stage < len(row_bits):
            target = (layer, flip(r, row_bits[stage]), c)
        else:
            target = (layer, r, flip(c, col_bits[stage - len(row_bits)]))
        return pltpu.make_async_remote_copy(
            src_ref=own_ref if stage == 0 else held.at[pl.ds(0, size)],
            dst_ref=held.at[1] if stage == 0 else held.at[pl.ds(size, size)],
            send_sem=send_sem.at[stage],
            recv_sem=recv_sem.at[stage],
            device_id=target,
            device_id_type=MESH,
        )

    def stage_copies(stage):
        return (
            spread(stage, levv, level_ref, lev_send, lev_recv),
            spread(stage, calv, cal_ref, cal_send, cal_recv),
        )

    own_copies = (
        pltpu.make_async_copy(level_ref, levv.at[0], lev_own),
        pltpu.make_async_copy(cal_ref, calv.at[0], cal_own),
    )

    def advance(stage):
        if stage >= stages:
            return
        if stage == 0:
            for copy in own_copies:
                copy.wait()
        for copy in stage_copies(stage):
            copy.wait_recv()
        if stage + 1 < stages:
            for copy in stage_copies(stage + 1):
                copy.start()

    barrier = pltpu.get_barrier_semaphore()

    @pl.loop(1, n)
    def _(i):
        target, _ = peer(i)
        pl.semaphore_signal(barrier, inc=1, device_id=target, device_id_type=MESH)

    sign_copies = [
        pltpu.make_async_copy(si_hbm, si_ref, sign_sem.at[0]),
        pltpu.make_async_copy(so_hbm, so_ref, sign_sem.at[1]),
    ]
    for copy in sign_copies:
        copy.start()
    for copy in own_copies:
        copy.start()
    for q in range(WEIGHT_SLOTS - 1):
        w_copy(q).start()
    pl.semaphore_wait(barrier, n - 1)

    if stages:
        for copy in stage_copies(0):
            copy.start()

    table = sylvester(BLK)
    table_b = table.astype(jnp.bfloat16)
    diagonal = lax.broadcasted_iota(jnp.int32, (BLK, BLK), 0) == lax.broadcasted_iota(jnp.int32, (BLK, BLK), 1)

    for copy in sign_copies:
        copy.wait()

    def static_sign(a, b):
        return 1.0 - 2.0 * (bin(a & b).count("1") & 1)

    @pl.loop(0, ib)
    def _(k):
        for g in range(groups):
            signs = si_ref[k, :, g * BLK : (g + 1) * BLK].astype(jnp.float32)
            scaled = jnp.where(diagonal, signs, 0.0).astype(jnp.bfloat16)
            skin[k, g * BLK : (g + 1) * BLK, :] = jnp.dot(
                scaled, table_b, preferred_element_type=jnp.float32
            ).astype(jnp.bfloat16)

    @pl.loop(0, ob)
    def _(j):
        for g in range(groups):
            signs = so_ref[j, :, g * BLK : (g + 1) * BLK].astype(jnp.float32)
            plus = (table * signs).astype(jnp.bfloat16)
            minus = (table * -signs).astype(jnp.bfloat16)
            for h in range(groups):
                kout[j, h * BLK : (h + 1) * BLK, g * BLK : (g + 1) * BLK] = plus if static_sign(g, h) > 0 else minus

    def inner(t, slot):
        for g in range(groups):
            parity = 0
            for bit in bits_of(groups):
                if g & bit:
                    parity = parity + lax.rem(t // bit, 2)
            sign = (1 - 2 * lax.rem(parity + 0 * t, 2)).astype(jnp.float32)
            for k in range(ib):
                rows = slice(g * BLK, (g + 1) * BLK)
                kin[k, rows, :] = (skin[k, rows, :].astype(jnp.float32) * sign).astype(jnp.bfloat16)

        @pl.loop(0, ob)
        def _(j):
            @pl.loop(0, ib)
            def _(k):
                q = (t * ob + j) * ib + k
                w_copy(q).wait()

                @pl.when(q + WEIGHT_SLOTS - 1 < chunks * blocks)
                def _():
                    w_copy(q + WEIGHT_SLOTS - 1).start()

                wslot = lax.rem(q, WEIGHT_SLOTS)

                @pl.loop(0, INNER // GROUP)
                def _(m):
                    rows = pl.ds(pl.multiple_of(m * GROUP, GROUP), GROUP)
                    cols = pl.ds(pl.multiple_of(k * BLK, BLK), BLK)
                    right[rows, cols] = jnp.dot(
                        wbuf[wslot, rows, :], kin[k], preferred_element_type=jnp.float32
                    ).astype(jnp.bfloat16)

            @pl.loop(0, INNER // GROUP)
            def _(m):
                rows = pl.ds(pl.multiple_of(m * GROUP, GROUP), GROUP)
                both = jnp.dot(kout[j, rows, :], right[...], preferred_element_type=jnp.float32)
                per = GROUP // pr
                sbuf[slot, pl.ds(m * per, per), :, j] = both.reshape(per, S, ds, wide).astype(jnp.bfloat16)

    def send(t, slot):
        @pl.loop(0, S)
        def _(s):
            u = t * S + s
            pltpu.make_async_copy(sbuf.at[slot, me, s], recv_ref.at[u, me], own_sem.at[slot]).start()

            @pl.loop(1, n)
            def _(i):
                target, place = peer(mixed_order(n, i))
                pltpu.make_async_remote_copy(
                    src_ref=sbuf.at[slot, place, s], dst_ref=recv_ref.at[u, me],
                    send_sem=ssem.at[slot], recv_sem=rsem.at[u],
                    device_id=target, device_id_type=MESH,
                ).start()

    def wait_send(slot):
        sent = sbuf.at[slot, pl.ds(0, n - 1)]
        pltpu.make_async_copy(sent, sent, ssem.at[slot]).wait()

    def wait_own(slot):
        own = sbuf.at[slot, me]
        pltpu.make_async_copy(own, own, own_sem.at[slot]).wait()

    d_block = me * pr // BLK
    d_blocks = INNER // BLK

    def read_levels():
        level = levv[...].astype(jnp.float32).reshape(n * ob, d_blocks, lev_cols)
        line = lax.broadcasted_iota(jnp.int32, level.shape, 1)
        level = jnp.sum(jnp.where(line == d_block, level, 0.0), axis=1, keepdims=True)
        level = jnp.broadcast_to(level, (n * ob, d_blocks, lev_cols)).reshape(n * ob * d_blocks, lev_cols)
        levb[...] = level.astype(jnp.bfloat16)

    def finish(h):
        own_units = range(h * (S // H), (h + 1) * (S // H))
        rows_each = ostage.shape[2]
        for s in own_units:
            accb[s] = (acc[s] * (1.0 / D)).astype(jnp.bfloat16)

        @pl.loop(0, R)
        def _(q):
            total = None
            for s in own_units:
                term = jnp.dot(accb[s], perm[q * S + s], preferred_element_type=jnp.float32)
                total = term if total is None else total + term
            for cc in range(C):
                ostage[h, q * C + cc] = total[cc * rows_each : (cc + 1) * rows_each].astype(jnp.bfloat16)

    def send_out(h):
        pltpu.make_async_copy(ostage.at[h, me], out_ref.at[h, me], out_recv.at[h]).start()

        @pl.loop(1, n)
        def _(i):
            target, place = peer(mixed_order(n, i))
            pltpu.make_async_remote_copy(
                src_ref=ostage.at[h, place], dst_ref=out_ref.at[h, me],
                send_sem=out_send.at[h], recv_sem=out_recv.at[h],
                device_id=target, device_id_type=MESH,
            ).start()

    def outer(t):
        lane = lax.broadcasted_iota(jnp.int32, (lev_cols, wide), 1)
        line = lax.broadcasted_iota(jnp.int32, (lev_cols, wide), 0)
        pick = jnp.where(line == (lane >> 7) * d_blocks + t, float(D // LEVEL_UNIT), 0.0).astype(jnp.bfloat16)
        lim[...] = jnp.dot(levb[...], pick, preferred_element_type=jnp.float32).reshape(lim.shape)

        @pl.loop(0, S)
        def _(s):
            u = t * S + s
            final_unit = (t == last) & (s == S - 1)
            if H > 1:
                @pl.when(final_unit)
                def _():
                    finish(0)

            arrived = recv_ref.at[u, pl.ds(0, n - 1)]
            pltpu.make_async_copy(arrived, arrived, rsem.at[u]).wait()
            if H > 1:
                @pl.when(final_unit)
                def _():
                    send_out(0)

            fetch = pltpu.make_async_copy(recv_ref.at[u], rbuf, usem)
            fetch.start()
            fetch.wait()

            @pl.loop(0, ai)
            def _(i):
                cc, k = i // ib, lax.rem(i, ib)
                cols = pl.ds(pl.multiple_of(k * BLK, BLK), BLK)
                mixed = butterfly(
                    rbuf[rr * C + cc, j, :, cols].astype(jnp.float32) for rr in range(R) for j in range(ob)
                )
                for o in range(ao):
                    mix[i, o] = mixed[o]

            @pl.loop(0, ao)
            def _(o):
                rr, j = o // ob, lax.rem(o, ob)
                slots = [held_slot(rr, cc) for cc in range(C)]
                mixed = butterfly(mix[i, o] for i in range(ai))
                for i in range(ai):
                    cc, k = i // ib, i % ib
                    limit = lim[slots[cc] * ob + j, :, k * BLK : (k + 1) * BLK]
                    value = mixed[i].reshape(ds // d_blocks, d_blocks, BLK)
                    value = jnp.minimum(jnp.maximum(value, -limit), limit)
                    clip[i, o] = value.reshape(ds, BLK).astype(jnp.bfloat16)

            total = None
            for i in range(ai):
                cc, k = i // ib, i % ib
                cols = pl.ds(pl.multiple_of(k * INNER + t * BLK, BLK), BLK)
                cal = jnp.concatenate([calv[held_slot(rr, cc), :, cols] for rr in range(R)], axis=0)
                term = lax.dot_general(
                    cal, clip[i].reshape(ao * ds, BLK), (((1,), (1,)), ((), ())), preferred_element_type=jnp.float32
                )
                total = term if total is None else total + term
            acc[s] += total

    spot = lax.broadcasted_iota(jnp.int32, perm.shape[1:], 0)
    lane = lax.broadcasted_iota(jnp.int32, perm.shape[1:], 1)
    shift = (pr // H).bit_length() - 1
    step = ds.bit_length() - 1
    for q in range(R):
        for s in range(S):
            turn = lax.rem(me, ob // H) * H + s // (S // H) if perm.shape[2] == BLK else 0
            wanted = (q * ob + (((lane >> shift) + ob - turn) & (ob - 1))) * ds + (lane & (ds - 1))
            hit = (spot == wanted) & (((lane & (pr // H - 1)) >> step) == s % (S // H))
            perm[q * S + s] = jnp.where(hit, 1.0, 0.0).astype(jnp.bfloat16)
    acc[...] = jnp.zeros_like(acc)

    @pl.loop(0, chunks + SEND_SLOTS)
    def _(i):
        slot = lax.rem(i, SEND_SLOTS)

        @pl.when(i >= SEND_SLOTS)
        def _():
            wait_own(slot)

        @pl.when(i < chunks)
        def _():
            @pl.when(i >= SEND_SLOTS)
            def _():
                wait_send(slot)

            inner(i, slot)
            send(i, slot)

        for at in range(SEND_SLOTS + 1):
            @pl.when(i == at)
            def _():
                advance(at)
                if at == SEND_SLOTS:
                    for later in range(at + 1, stages):
                        advance(later)
                    read_levels()

        @pl.when(i >= SEND_SLOTS)
        def _():
            outer(i - SEND_SLOTS)

    finish(H - 1)
    send_out(H - 1)

    for t in range(chunks - SEND_SLOTS, chunks):
        wait_send(t % SEND_SLOTS)
    for stage in range(stages):
        for copy in stage_copies(stage):
            copy.wait_send()
    for h in range(H):
        pltpu.make_async_copy(out_ref.at[h], out_ref.at[h], out_recv.at[h]).wait()
        sent = ostage.at[h, pl.ds(0, n - 1)]
        pltpu.make_async_copy(sent, sent, out_send.at[h]).wait()


def merge_kernel(ob, x_ref, o_ref):
    H, n, rows, _ = x_ref.shape
    width = BLK // ob
    joined = ob // H
    tiles = n // joined
    slot = lax.broadcasted_iota(jnp.int32, (rows, BLK), 1) // width
    for at in range(tiles):
        values = [x_ref[k % H, at * joined + k // H].astype(jnp.float32) for k in range(ob)]
        for j in range(ob):
            merged = values[0]
            for k in range(1, ob):
                merged = jnp.where(slot == (j + k) % ob, values[k], merged)
            if j:
                merged = pltpu.roll(merged, BLK - j * width, 1)
            cols = slice((j * tiles + at) * BLK, (j * tiles + at + 1) * BLK)
            o_ref[:, cols] = merged.astype(jnp.bfloat16)


def shards(query_weight, sign_input, sign_output, clip_level, calibration):
    rows_local, cols_local = query_weight.shape
    R, C = lax.axis_size("row"), lax.axis_size("col")
    n = R * C
    ob, ib = rows_local // INNER, cols_local // INNER
    pr = INNER // n
    ds = min(16, pr)
    S = pr // ds
    H = 2 if S % 2 == 0 else 1
    chunks = INNER // BLK
    cal_local = calibration.shape[0]
    cal_rows = R * cal_local
    ao, ai = R * ob, C * ib
    wide = ib * BLK
    stages = len(bits_of(R)) + len(bits_of(C))
    bf16, f32 = jnp.bfloat16, jnp.float32

    _, result = pl.pallas_call(
        functools.partial(kernel, R, C),
        in_specs=[
            pl.BlockSpec(memory_space=pl.ANY),
            pl.BlockSpec(memory_space=pl.ANY),
            pl.BlockSpec(memory_space=pl.ANY),
            pl.BlockSpec(memory_space=pl.ANY),
            pl.BlockSpec(memory_space=pl.ANY),
        ],
        out_specs=[pl.BlockSpec(memory_space=pl.ANY)] * 2,
        out_shape=[
            jax.ShapeDtypeStruct((chunks * S, n, ob, ds, wide), bf16),
            jax.ShapeDtypeStruct((H, n, cal_rows // C, ob * pr // H), bf16),
        ],
        scratch_shapes=[
            pltpu.VMEM((ib, 1, INNER), jnp.int32),
            pltpu.VMEM((ob, 1, INNER), jnp.int32),
            pltpu.VMEM((ob, INNER, INNER), bf16),
            pltpu.VMEM((ib, INNER, BLK), bf16),
            pltpu.VMEM((ib, INNER, BLK), bf16),
            pltpu.VMEM((WEIGHT_SLOTS, INNER, INNER), bf16),
            pltpu.VMEM((INNER, wide), bf16),
            pltpu.VMEM((SEND_SLOTS, n, S, ob, ds, wide), bf16),
            pltpu.VMEM((n, ob, ds, wide), bf16),
            pltpu.VMEM((ai, ao, ds, BLK), f32),
            pltpu.VMEM((ai, ao, ds, BLK), bf16),
            pltpu.VMEM((S, cal_rows, ao * ds), f32),
            pltpu.VMEM((S, cal_rows, ao * ds), bf16),
            pltpu.VMEM((R * S, ao * ds, ob * pr // H), bf16),
            pltpu.VMEM((n, cal_local, cols_local), bf16),
            pltpu.VMEM((n,) + clip_level.shape, jnp.int32),
            pltpu.VMEM((n * clip_level.shape[0], clip_level.shape[1]), bf16),
            pltpu.VMEM((n * ob, INNER // BLK, wide), f32),
            pltpu.VMEM((H, n, cal_rows // C, ob * pr // H), bf16),
            pltpu.SemaphoreType.DMA((2,)),
            pltpu.SemaphoreType.DMA((WEIGHT_SLOTS,)),
            pltpu.SemaphoreType.DMA((SEND_SLOTS,)),
            pltpu.SemaphoreType.DMA((SEND_SLOTS,)),
            pltpu.SemaphoreType.DMA((chunks * S,)),
            pltpu.SemaphoreType.DMA,
            pltpu.SemaphoreType.DMA,
            pltpu.SemaphoreType.DMA((max(stages, 1),)),
            pltpu.SemaphoreType.DMA((max(stages, 1),)),
            pltpu.SemaphoreType.DMA,
            pltpu.SemaphoreType.DMA((max(stages, 1),)),
            pltpu.SemaphoreType.DMA((max(stages, 1),)),
            pltpu.SemaphoreType.DMA((H,)),
            pltpu.SemaphoreType.DMA((H,)),
        ],
        compiler_params=pltpu.CompilerParams(
            collective_id=0, has_side_effects=True, vmem_limit_bytes=60 * 2**20
        ),
    )(query_weight, sign_input.reshape(ib, 1, INNER), sign_output.reshape(ob, 1, INNER), clip_level, calibration)

    rows_out = cal_rows // C
    if ob * pr // H == BLK:
        block = rows_out // 2 if rows_out % 32 == 0 else rows_out
        return pl.pallas_call(
            functools.partial(merge_kernel, ob),
            grid=(rows_out // block,),
            in_specs=[pl.BlockSpec((H, n, block, BLK), lambda i: (0, 0, i, 0))],
            out_specs=pl.BlockSpec((block, rows_local), lambda i: (i, 0)),
            out_shape=jax.ShapeDtypeStruct((rows_out, rows_local), bf16),
        )(result)
    result = result.reshape(H, n, rows_out, ob, pr // H)
    return result.transpose(2, 3, 1, 0, 4).reshape(rows_out, rows_local)


def solution(mesh):
    placed = (
        P(("layer", "row"), "col"),
        P(("layer", "col")),
        P(("layer", "row")),
        P(("layer", "row"), "col"),
        P(("layer", "row"), "col"),
    )
    return jax.shard_map(
        shards, mesh=mesh, in_specs=placed, out_specs=P(("layer", "col"), "row"), check_vma=False
    )
```
